512 devices in a mesh: ctx: 64 (over z_lo, y, core), head: 8 (over x, z_hi).
Axes of the slice: x: 4, y: 8, z: 8 (z_hi: 2, z_lo: 4; z = z_hi * 4 + z_lo), core: 2. Of those that a mesh axis runs over, the one named last changes fastest.
Arguments:
- tokens: bfloat16 [32768, 3840], P('ctx', 'head'), may hold values from -18 to 18
- w_query: bfloat16 [3840, 4096], P('ctx', 'head'), may hold values from -0.09375 to 0.09375
- key_matrix: bfloat16 [3840, 2048], P('ctx', 'head'), may hold values from -0.09375 to 0.09375
- value_matrix: bfloat16 [3840, 2048], P('ctx', 'head'), may hold values from -0.09375 to 0.09375
- d_attended: bfloat16 [32768, 4096], P('ctx', 'head'), may hold values from -6 to 6
- doc_lengths: int32 [32], replicated, may hold values from 1 to 2048, 32768 in all
Outputs:
- attended: bfloat16 [32768, 4096], P('ctx', 'head')
- key_grad: bfloat16 [32768, 2048], P('ctx', 'head')
The draws below stay inside these ranges and needn't reach their ends.
Inputs may be any that keep to these rules, and one draw needn't show every extreme that they name: `doc_lengths`: the documents lie end to end from position 0 and fill all 32768 positions.
All inputs are finite; a program needn't handle non-finite values.
Results may differ from the reference program's by a relative error of at most 0.012.
The reference program's roundings to bfloat16 on the way (of `query`, `probs_low` and `dscore`) count: a program that leaves them out, or rounds other values in their place, can miss the bound.
Values may be sent and summed in bfloat16 or wider, within the bound.
No kernel may reach another device: no remote copies, remote signals or barrier semaphores. Data moves between devices by JAX's collectives and lax.ppermute only.
A program may use at most 64 MiB of HBM per device.

```python
import math
import jax
import jax.numpy as jnp
import numpy as np
from jax import lax

MODEL_WIDTH = 3840
HQ = 16
KEY_VALUE_HEADS = 8
HEAD_SIZE = 256
WINDOW = 1024
TOK_DEV = 512
CONTEXT_TOKENS = 32768
DOCS = 32


def draw_tokens(key, part):
    values = jax.random.truncated_normal(key, -6.0, 6.0, (CONTEXT_TOKENS, MODEL_WIDTH), jnp.float32)
    return values.astype(jnp.bfloat16)


def block_scale(rng, shape, pieces, smallest, high):
    loudness = 1.0
    for position, shards_of in pieces:
        heights = jax.random.uniform(jax.random.fold_in(jax.random.fold_in(rng, 6), position), (shards_of,), jnp.float32, smallest / len(pieces), high / len(pieces))
        loudness = loudness * jnp.repeat(jnp.exp(heights), shape[position] // shards_of).reshape((-1,) + (1,) * (len(shape) - 1 - position))
    return loudness


def profile(count, total, limit, lean):
    weights = [(1 << 20) // math.isqrt(standing ** lean) + 1 for standing in range(2, count + 1)]
    rest, counts = total - limit - (count - 1), [1] * (count - 1)
    while rest > 0:
        candidates = [i for i in range(count - 1) if counts[i] < limit]
        mass, remaining = sum([weights[i] for i in candidates]), rest
        for i in candidates:
            addition = min(limit - counts[i], max(1, remaining * weights[i] // mass), rest)
            counts[i] = counts[i] + addition
            rest = rest - addition
    return np.array([limit] + counts)


def uneven_parts(own_key, count, total, limit, skew):
    if count == 2:
        one = jax.random.randint(own_key, (), max(1, total - limit), min(limit, total - 1) + 1)
        return jnp.stack([one, total - one])
    sizes = jnp.asarray(profile(count, total, limit, skew), jnp.int32)
    twos = (count - 1) // 2
    giver, taker = sizes[1:1 + 2 * twos:2], sizes[2:2 + 2 * twos:2]
    margin = jnp.minimum(giver - 1, limit - taker)
    passed = jax.random.randint(jax.random.fold_in(own_key, 1), (twos,), 0, 1 << 20) % (margin + 1)
    sizes = sizes.at[1:1 + 2 * twos:2].set(giver - passed).at[2:2 + 2 * twos:2].set(taker + passed)
    return sizes[jax.random.permutation(jax.random.fold_in(own_key, 2), count)]


def noise(key, shape, deviation, most, pieces=(), held_as=jnp.bfloat16):
    result = deviation * jax.random.normal(key, shape, jnp.float32)
    if pieces:
        result = result * block_scale(key, shape, pieces, -0.22, 0.18)
    return jnp.clip(result, -most, most).astype(held_as)


def setup_inputs(seed: int = 0) -> dict:
    splits = jax.random.split(jax.random.key(seed), 7)
    return {
        "tokens": draw_tokens(jax.random.fold_in(splits[6], 71), 0),
        "w_query": noise(splits[1], (MODEL_WIDTH, HQ * HEAD_SIZE), MODEL_WIDTH ** -0.5, 0.09375, ((0, 64), (1, 8))),
        "key_matrix": noise(splits[2], (MODEL_WIDTH, KEY_VALUE_HEADS * HEAD_SIZE), MODEL_WIDTH ** -0.5, 0.09375, ((0, 64), (1, 8))),
        "value_matrix": noise(splits[3], (MODEL_WIDTH, KEY_VALUE_HEADS * HEAD_SIZE), MODEL_WIDTH ** -0.5, 0.09375, ((0, 64), (1, 8))),
        "d_attended": noise(splits[4], (CONTEXT_TOKENS, HQ * HEAD_SIZE), 1.0, 6.0, ((0, 64), (1, 8))),
        "doc_lengths": uneven_parts(splits[5], DOCS, CONTEXT_TOKENS, 2 * WINDOW, 2).astype(jnp.int32),
    }


def doc_begin(positions, doc_start):
    inside = doc_start[None, :] <= positions[:, None]
    return jnp.max(jnp.where(inside, doc_start[None, :], 0), axis=1)


def attend_block(query_blk, key_block, value_block, grad_blk, leading_row, doc_start):
    rows = query_blk.shape[0]
    window_length = key_block.shape[0]
    kv_heads = key_block.shape[1]
    group = query_blk.shape[1] // kv_heads
    width = query_blk.shape[2]
    query_pos = leading_row + jnp.arange(rows, dtype=jnp.int32)
    key_pos = leading_row - (window_length - rows) + jnp.arange(window_length, dtype=jnp.int32)
    begins = doc_begin(query_pos, doc_start)
    allowed = (key_pos[None, :] >= begins[:, None]) & (key_pos[None, :] <= query_pos[:, None]) & (key_pos[None, :] > query_pos[:, None] - WINDOW)
    query_four = query_blk.reshape(rows, kv_heads, group, width).astype(jnp.float32)
    grad_four = grad_blk.reshape(rows, kv_heads, group, width).astype(jnp.float32)
    key_three = key_block.astype(jnp.float32)
    value_three = value_block.astype(jnp.float32)
    scores = jnp.einsum("tgeh,sgh->gets", query_four, key_three)
    scores = jnp.where(allowed[None, None], scores, -1e30)
    peak = jnp.max(scores, axis=-1, keepdims=True)
    expo = jnp.exp(scores - peak)
    probs = expo / jnp.sum(expo, axis=-1, keepdims=True)
    probs_low = probs.astype(jnp.bfloat16)
    attended = jnp.einsum("gets,sgh->tgeh", probs_low.astype(jnp.float32), value_three)
    attended = attended.astype(jnp.bfloat16).reshape(rows, kv_heads * group * width)
    dprob = jnp.einsum("tgeh,sgh->gets", grad_four, value_three)
    delta = jnp.sum(probs * dprob, axis=-1, keepdims=True)
    dscore = (probs * (dprob - delta)).astype(jnp.bfloat16)
    key_part = jnp.einsum("gets,tgeh->sgh", dscore.astype(jnp.float32), query_four)
    return attended, key_part.reshape(window_length, kv_heads * width)


def reference(tokens, w_query, key_matrix, value_matrix, d_attended, doc_lengths):
    doc_start = (jnp.cumsum(doc_lengths) - doc_lengths).astype(jnp.int32)
    window_extent = (WINDOW // TOK_DEV) * TOK_DEV
    window_length = window_extent + TOK_DEV
    query = (jnp.dot(tokens, w_query, preferred_element_type=jnp.float32) * 0.0625).astype(jnp.bfloat16)
    keys = jnp.dot(tokens, key_matrix, preferred_element_type=jnp.float32).astype(jnp.bfloat16)
    values = jnp.dot(tokens, value_matrix, preferred_element_type=jnp.float32).astype(jnp.bfloat16)
    padded_keys = jnp.concatenate([jnp.zeros((window_extent, keys.shape[1]), jnp.bfloat16), keys], axis=0)
    padded_values = jnp.concatenate([jnp.zeros((window_extent, values.shape[1]), jnp.bfloat16), values], axis=0)

    def step(key_acc, block):
        leading_row = (block * TOK_DEV).astype(jnp.int32)
        query_blk = lax.dynamic_slice_in_dim(query, leading_row, TOK_DEV, 0).reshape(TOK_DEV, HQ, HEAD_SIZE)
        grad_blk = lax.dynamic_slice_in_dim(d_attended, leading_row, TOK_DEV, 0).reshape(TOK_DEV, HQ, HEAD_SIZE)
        key_block = lax.dynamic_slice_in_dim(padded_keys, leading_row, window_length, 0).reshape(window_length, KEY_VALUE_HEADS, HEAD_SIZE)
        value_block = lax.dynamic_slice_in_dim(padded_values, leading_row, window_length, 0).reshape(window_length, KEY_VALUE_HEADS, HEAD_SIZE)
        attended, key_part = attend_block(query_blk, key_block, value_block, grad_blk, leading_row, doc_start)
        current = lax.dynamic_slice_in_dim(key_acc, leading_row, window_length, 0)
        key_acc = lax.dynamic_update_slice_in_dim(key_acc, current + key_part, leading_row, 0)
        return key_acc, attended

    start_running = jnp.zeros((window_extent + CONTEXT_TOKENS, KEY_VALUE_HEADS * HEAD_SIZE), jnp.float32)
    key_acc, blocks_out = lax.scan(step, start_running, jnp.arange(CONTEXT_TOKENS // TOK_DEV, dtype=jnp.int32))
    attended = blocks_out.reshape(CONTEXT_TOKENS, HQ * HEAD_SIZE)
    key_grad = key_acc[window_extent:].astype(jnp.bfloat16)
    return attended, key_grad
```

```python
import jax
import jax.numpy as jnp
from jax import lax
from jax.experimental import pallas as pl
from jax.experimental.pallas import tpu as pltpu
from jax.sharding import PartitionSpec as P

HEAD_SIZE = 256
WINDOW = 1024
NX, NY, NZL, NZH = 4, 8, 4, 2
NZ = NZL * NZH
ROWS = 60
PAD = 64
PAIR = 2 * PAD
BOTH = ("ctx", "head")
BF = jnp.bfloat16
F32 = jnp.float32


def place(x, y, z, core):
    x, y, z = x % NX, y % NY, z % NZ
    ctx = (z % NZL) * 2 * NY + 2 * y + core
    return ctx * (NX * NZH) + x * NZH + z // NZL


def hop(block, dx=0, dy=0, dz=0, swap=0, by_core=False):
    route = []
    for x in range(NX):
        for y in range(NY):
            for z in range(NZ):
                for core in range(2):
                    s = 1 - 2 * core if by_core else 1
                    route.append(
                        (
                            place(x, y, z, core),
                            place(x + s * dx, y + s * dy, z + s * dz, core ^ swap),
                        )
                    )
    return lax.ppermute(block, BOTH, route)


def along_ctx(block, distance):
    n = lax.axis_size("ctx")
    route = [(i - distance, i) for i in range(n) if 0 <= i - distance < n]
    return lax.ppermute(block, "ctx", route)


def doc_begin(positions, doc_start):
    inside = doc_start[None, :] <= positions[:, None]
    return jnp.max(jnp.where(inside, doc_start[None, :], 0), axis=1)


def project_body(pos, t_ref, own_ref, r1, s1, r2, s2, r3, s3, r4, s4, o_ref, *, scale):
    x, y, zh, sign = pos[0], pos[1], pos[2], pos[3]
    total = jnp.zeros(o_ref.shape, F32)
    blocks = [(own_ref, 0, 0)]
    for z in range(NZL):
        slot_x = lax.rem(sign * (x - z) + NX, NX)

        def columns(ycoord):
            other = jnp.where(lax.div(ycoord, 4) == zh, 0, 4)
            at = pl.multiple_of(lax.rem(ycoord, 4) * PAIR, PAIR)
            return t_ref[slot_x + other, :, pl.ds(at, PAIR)]

        left, right = [], []
        for ref, d in ((own_ref, 0), (r1, -1), (s1, 1), (r2, -2), (s2, 2), (r3, -3), (s3, 3)):
            left.append(columns(lax.rem(y + sign * d + NY, NY)))
            right.append(ref[z])
        left.append(columns(lax.rem(y + 4, NY)))
        core = lax.div(1 - sign, 2)
        mine = r4[z % 2]
        theirs = s4[z % 2]
        first = jnp.where(core == 0, 1, 0)
        use = first if z < 2 else 1 - first
        right.append(jnp.where(use == 1, mine, theirs))
        total += jnp.dot(
            jnp.concatenate(left, axis=1),
            jnp.concatenate(right, axis=0),
            preferred_element_type=F32,
        )
    o_ref[...] = (total * scale).astype(BF)


def project(pos, tokens8, blocks, scale):
    rows = tokens8.shape[1]
    cols = blocks[0].shape[-1]
    full = pl.BlockSpec(memory_space=pltpu.VMEM)
    return pl.pallas_call(
        lambda *refs: project_body(*refs, scale=scale),
        out_shape=jax.ShapeDtypeStruct((rows, cols), BF),
        in_specs=[pl.BlockSpec(memory_space=pltpu.SMEM)] + [full] * 10,
        out_specs=full,
        cost_estimate=pl.CostEstimate(
            flops=2 * rows * 4096 * cols,
            bytes_accessed=2 * (rows * 4096 + cols * 4096 + rows * cols),
            transcendentals=0,
        ),
        compiler_params=pltpu.CompilerParams(vmem_limit_bytes=48 * 1024 * 1024),
        name="project",
    )(pos, tokens8, *blocks)


def ring_y(block, core):
    out = [block]
    now = block
    for step in range(3):
        now = hop(now, dy=1, by_core=True)
        out += [now, hop(now, swap=1)]
    half = jnp.where(core == 0, now[:2], now[2:])
    now = hop(half, dy=1, by_core=True)
    out += [now, hop(now, swap=1)]
    return out


def ring_x(block):
    out = [block]
    for step in range(3):
        out.append(hop(out[-1], dx=1, by_core=True))
    return out


def gather_zcore(w):
    groups = [
        [z * 2 * NY + 2 * y + core for z in range(NZL) for core in range(2)] for y in range(NY)
    ]
    got = lax.all_gather(w, "ctx", axis=0, tiled=True, axis_index_groups=groups)
    return got.reshape(NZL, PAIR, w.shape[1])


def attend_local(query, key_ext, value_ext, grad_rows, leading_row, doc_start, kv_heads):
    rows = query.shape[0]
    window_length = key_ext.shape[0]
    width = key_ext.shape[1] // kv_heads
    group = query.shape[1] // (kv_heads * width)
    query_pos = leading_row + jnp.arange(rows, dtype=jnp.int32)
    key_pos = leading_row - (window_length - rows) + jnp.arange(window_length, dtype=jnp.int32)
    begins = doc_begin(query_pos, doc_start)
    allowed = (
        (key_pos[None, :] >= begins[:, None])
        & (key_pos[None, :] <= query_pos[:, None])
        & (key_pos[None, :] > query_pos[:, None] - WINDOW)
    )
    query_four = query.reshape(rows, kv_heads, group, width)
    grad_four = grad_rows.reshape(rows, kv_heads, group, width)
    key_three = key_ext.reshape(window_length, kv_heads, width)
    value_three = value_ext.reshape(window_length, kv_heads, width)
    scores = jnp.einsum("tgeh,sgh->gets", query_four, key_three, preferred_element_type=F32)
    scores = jnp.where(allowed[None, None], scores, -1e30)
    peak = jnp.max(scores, axis=-1, keepdims=True)
    expo = jnp.exp(scores - peak)
    probs = expo / jnp.sum(expo, axis=-1, keepdims=True)
    probs_low = probs.astype(BF)
    attended = jnp.einsum("gets,sgh->tgeh", probs_low, value_three, preferred_element_type=F32)
    attended = attended.astype(BF).reshape(rows, kv_heads * group * width)
    dprob = jnp.einsum("tgeh,sgh->gets", grad_four, value_three, preferred_element_type=F32)
    delta = jnp.sum(probs * dprob, axis=-1, keepdims=True)
    dscore = (probs * (dprob - delta)).astype(BF)
    key_part = jnp.einsum("gets,tgeh->sgh", dscore, query_four, preferred_element_type=F32)
    return (attended, key_part.reshape(window_length, kv_heads * width))


def local(tokens, w_query, key_matrix, value_matrix, d_attended, doc_lengths):
    rows = tokens.shape[0]
    ctx = lax.axis_index("ctx").astype(jnp.int32)
    head = lax.axis_index("head").astype(jnp.int32)
    core, y = ctx % 2, (ctx // 2) % NY
    x, zh = head // NZH, head % NZH
    pos = jnp.stack([x, y, zh, 1 - 2 * core])

    feature = jnp.arange(tokens.shape[1], dtype=jnp.int32)
    target = feature // ROWS * PAD + feature % ROWS
    spread = (target[:, None] == jnp.arange(8 * PAD, dtype=jnp.int32)[None, :]).astype(BF)
    own = jnp.dot(tokens, spread, preferred_element_type=F32).astype(BF)

    fill = ((0, PAD - ROWS), (0, 0))
    w_kv = jnp.pad(jnp.concatenate([key_matrix, value_matrix], axis=1), fill)
    w_q = jnp.pad(w_query, fill)

    partner = hop(own, dz=NZL)
    b_kv = gather_zcore(w_kv)
    b_q = gather_zcore(w_q)
    tokens8 = jnp.stack(ring_x(own) + ring_x(partner))
    kv_blocks = ring_y(b_kv, core)
    q_blocks = ring_y(b_q, core)

    joined = project(pos, tokens8, kv_blocks, 1.0)
    query = project(pos, tokens8, q_blocks, 0.0625)

    blocks = WINDOW // rows
    earlier = [along_ctx(joined, distance) for distance in range(blocks, 0, -1)]
    extended = jnp.concatenate(earlier + [joined], axis=0)
    doc_start = jnp.cumsum(doc_lengths) - doc_lengths
    leading_row = ctx * rows
    attended, key_part = attend_local(
        query,
        extended[:, :HEAD_SIZE],
        extended[:, HEAD_SIZE:],
        d_attended,
        leading_row,
        doc_start,
        1,
    )

    def share(distance):
        begin = (blocks - distance) * rows
        return key_part[begin : begin + rows]

    key_total = share(0)
    for distance in range(1, blocks + 1):
        key_total = key_total + along_ctx(share(distance).astype(BF), -distance).astype(F32)
    return (attended, key_total.astype(BF))


def solution(mesh):
    return jax.shard_map(
        local,
        mesh=mesh,
        in_specs=(
            P("ctx", "head"),
            P("ctx", "head"),
            P("ctx", "head"),
            P("ctx", "head"),
            P("ctx", "head"),
            P(),
        ),
        out_specs=(P("ctx", "head"), P("ctx", "head")),
        check_vma=False,
    )
```

```python
import jax
import jax.numpy as jnp
from jax import lax
from jax.experimental import pallas as pl
from jax.experimental.pallas import tpu as pltpu
from jax.sharding import PartitionSpec as P


HEAD_SIZE = 256
WINDOW = 1024
NX, NY, NZL, NZH = 4, 8, 4, 2
NZ = NZL * NZH
ROWS = 60
PAD = 64
PAIR = 2 * PAD
BOTH = ("ctx", "head")
BF = jnp.bfloat16
F32 = jnp.float32


def place(x, y, z, core):
    x, y, z = x % NX, y % NY, z % NZ
    ctx = (z % NZL) * 2 * NY + 2 * y + core
    return ctx * (NX * NZH) + x * NZH + z // NZL


def hop(block, dx=0, dy=0, dz=0, swap=0, by_core=False):
    route = []
    for x in range(NX):
        for y in range(NY):
            for z in range(NZ):
                for core in range(2):
                    s = 1 - 2 * core if by_core else 1
                    route.append(
                        (
                            place(x, y, z, core),
                            place(x + s * dx, y + s * dy, z + s * dz, core ^ swap),
                        )
                    )
    return lax.ppermute(block, BOTH, route)


def along_ctx(block, distance):
    n = lax.axis_size("ctx")
    route = [(i - distance, i) for i in range(n) if 0 <= i - distance < n]
    return lax.ppermute(block, "ctx", route)


def project_body(pos, t0, t1, t2, t3, p0, p1, p2, p3, *refs, scale, swaps):
    *blocks, o_ref = refs
    own_ref, r1, r2, r3, r4 = blocks[:5]
    swapped = blocks[5:]
    x, y, zh, sign, core = pos[0], pos[1], pos[2], pos[3], pos[4]
    total = jnp.zeros(o_ref.shape, F32)

    def back(step, z):
        ref, at = swaps[step - 1]
        return swapped[ref][at + z]

    for slot, (near, far) in enumerate(((t0, p0), (t1, p1), (t2, p2), (t3, p3))):
        z = lax.rem(x - sign * slot + NX, NX)
        half = lax.rem(z, 2)

        def columns(distance):
            chip = lax.rem(y + sign * distance + NY, NY)
            at = pl.multiple_of(lax.rem(chip, 4) * PAIR, PAIR)
            return jnp.where(lax.div(chip, 4) == zh, near[:, pl.ds(at, PAIR)], far[:, pl.ds(at, PAIR)])

        left = [columns(d) for d in (0, 4, -1, 1, -2, 2, -3, 3)]
        right = [own_ref[z], jnp.where(lax.div(z, 2) == core, r4[half], back(4, half))]
        for step, ref in ((1, r1), (2, r2), (3, r3)):
            right += [ref[z], back(step, z)]
        total += jnp.dot(
            jnp.concatenate(left, axis=1),
            jnp.concatenate(right, axis=0),
            preferred_element_type=F32,
        )
    o_ref[...] = (total * scale).astype(BF)


def project(pos, near, far, ring, swapped, swaps, scale):
    rows = near[0].shape[0]
    cols = ring[0].shape[-1]
    full = pl.BlockSpec(memory_space=pltpu.VMEM)
    operands = [*near, *far, *ring, *swapped]
    return pl.pallas_call(
        lambda *refs: project_body(*refs, scale=scale, swaps=swaps),
        out_shape=jax.ShapeDtypeStruct((rows, cols), BF),
        in_specs=[pl.BlockSpec(memory_space=pltpu.SMEM)] + [full] * len(operands),
        out_specs=full,
        cost_estimate=pl.CostEstimate(
            flops=2 * rows * 4096 * cols,
            bytes_accessed=2 * (rows * 4096 + cols * 4096 + rows * cols),
            transcendentals=0,
        ),
        compiler_params=pltpu.CompilerParams(vmem_limit_bytes=48 * 1024 * 1024),
        name="project",
    )(pos, *operands)


def ring_y(block, core):
    out = [block]
    for _ in range(3):
        out.append(hop(out[-1], dy=1, by_core=True))
    half = lax.dynamic_slice_in_dim(out[-1], 2 * core, 2, 0)
    out.append(hop(half, dy=1, by_core=True))
    return out


def ring_x(block):
    out = [block]
    for _ in range(3):
        out.append(hop(out[-1], dx=1, by_core=True))
    return out


def gather_zcore(w):
    groups = [
        [z * 2 * NY + 2 * y + core for z in range(NZL) for core in range(2)] for y in range(NY)
    ]
    return lax.all_gather(w, "ctx", axis=0, tiled=False, axis_index_groups=groups)


TILE = 256
REACH = 5 * TILE


def scores_body(lead, len_ref, q_ref, own, e1, e2, g_ref, p_ref, dk0, dk1, dk2, ext, s_ref, d_ref, acc):
    rows = q_ref.shape[0]
    ext[0:rows] = e2[...]
    ext[rows : 2 * rows] = e1[...]
    ext[2 * rows : 3 * rows] = own[...]
    acc[...] = jnp.zeros_like(acc)
    docs = len_ref.shape[1]
    i0 = lax.broadcasted_iota(jnp.int32, (docs, docs), 0)
    i1 = lax.broadcasted_iota(jnp.int32, (docs, docs), 1)
    starts = jnp.sum(jnp.where(i1 < i0, len_ref[...], 0), axis=1, keepdims=True)

    @pl.loop(0, 4)
    def _(step):
        i, h = lax.rem(step, 2), lax.div(step, 2)
        row0 = pl.multiple_of(i * TILE, TILE)
        col0 = pl.multiple_of(h * HEAD_SIZE, HEAD_SIZE)
        q = q_ref[pl.ds(row0, TILE), pl.ds(col0, HEAD_SIZE)]
        g = g_ref[pl.ds(row0, TILE), pl.ds(col0, HEAD_SIZE)]
        row = row0 + lax.broadcasted_iota(jnp.int32, (1, TILE), 1)
        at = lead[0] + row
        begin = jnp.max(jnp.where(starts <= at, starts, 0), axis=0, keepdims=True)
        low = jnp.maximum(begin - lead[0] + WINDOW, row + 1)
        nt = (((1,), (1,)), ((), ()))
        peak = jnp.full((1, TILE), -1e30, F32)
        for j in range(5):
            first = pl.multiple_of(row0 + j * TILE, TILE)
            s = lax.dot_general(ext[pl.ds(first, TILE), :HEAD_SIZE], q, nt, preferred_element_type=F32)
            key = first + lax.broadcasted_iota(jnp.int32, (TILE, 1), 0)
            ok = key >= low
            if j == 4:
                ok = ok & (key <= row + WINDOW)
            s = jnp.where(ok, s, -1e30)
            s_ref[j * TILE : (j + 1) * TILE] = s
            peak = jnp.maximum(peak, jnp.max(s, axis=0, keepdims=True))
        total = jnp.zeros((1, TILE), F32)
        for j in range(5):
            e = jnp.exp(s_ref[j * TILE : (j + 1) * TILE] - peak)
            s_ref[j * TILE : (j + 1) * TILE] = e
            total += jnp.sum(e, axis=0, keepdims=True)
        inverse = 1.0 / total
        delta = jnp.zeros((1, TILE), F32)
        for j in range(5):
            first = pl.multiple_of(row0 + j * TILE, TILE)
            d = lax.dot_general(ext[pl.ds(first, TILE), HEAD_SIZE:], g, nt, preferred_element_type=F32)
            p = s_ref[j * TILE : (j + 1) * TILE] * inverse
            s_ref[j * TILE : (j + 1) * TILE] = p
            d_ref[j * TILE : (j + 1) * TILE] = d
            p_ref[step, j * TILE : (j + 1) * TILE] = p.astype(BF)
            delta += jnp.sum(p * d, axis=0, keepdims=True)
        for j in range(5):
            first = pl.multiple_of(row0 + j * TILE, TILE)
            part = slice(j * TILE, (j + 1) * TILE)
            ds = (s_ref[part] * (d_ref[part] - delta)).astype(BF)
            acc[pl.ds(first, TILE)] += jnp.dot(ds, q, preferred_element_type=F32)

    dk2[...] = acc[0:rows].astype(BF)
    dk1[...] = acc[rows : 2 * rows].astype(BF)
    dk0[...] = acc[2 * rows : 3 * rows]


def values_body(p_ref, own, e1, e2, o_ref):
    tn = (((0,), (0,)), ((), ()))
    for i in range(2):
        value = jnp.concatenate(
            [e2[i * TILE :, HEAD_SIZE:], e1[:, HEAD_SIZE:], own[: (i + 1) * TILE, HEAD_SIZE:]], axis=0
        )
        for h in range(2):
            a = lax.dot_general(p_ref[2 * h + i], value, tn, preferred_element_type=F32)
            o_ref[i * TILE : (i + 1) * TILE, h * HEAD_SIZE : (h + 1) * HEAD_SIZE] = a.astype(BF)


def attend(lead, lens, query, own, e1, e2, grad):
    rows = query.shape[0]
    full = pl.BlockSpec(memory_space=pltpu.VMEM)
    smem = pl.BlockSpec(memory_space=pltpu.SMEM)
    shape = jax.ShapeDtypeStruct
    pairs = 4 * TILE * REACH
    p, dk0, dk1, dk2 = pl.pallas_call(
        scores_body,
        out_shape=(
            shape((4, REACH, TILE), BF),
            shape((rows, HEAD_SIZE), F32),
            shape((rows, HEAD_SIZE), BF),
            shape((rows, HEAD_SIZE), BF),
        ),
        in_specs=[smem] + [full] * 6,
        out_specs=(full,) * 4,
        scratch_shapes=[
            pltpu.VMEM((3 * rows, 2 * HEAD_SIZE), BF),
            pltpu.VMEM((REACH, TILE), F32),
            pltpu.VMEM((REACH, TILE), F32),
            pltpu.VMEM((3 * rows, HEAD_SIZE), F32),
        ],
        cost_estimate=pl.CostEstimate(
            flops=6 * pairs * HEAD_SIZE, bytes_accessed=5 * rows * 1024 + 2 * pairs, transcendentals=pairs
        ),
        compiler_params=pltpu.CompilerParams(vmem_limit_bytes=48 * 1024 * 1024),
        name="scores",
    )(lead, lens, query, own, e1, e2, grad)
    out = pl.pallas_call(
        values_body,
        out_shape=shape((rows, 2 * HEAD_SIZE), BF),
        in_specs=[full] * 4,
        out_specs=full,
        cost_estimate=pl.CostEstimate(
            flops=2 * pairs * HEAD_SIZE, bytes_accessed=4 * rows * 1024 + 2 * pairs, transcendentals=0
        ),
        compiler_params=pltpu.CompilerParams(vmem_limit_bytes=48 * 1024 * 1024),
        name="values",
    )(p, own, e1, e2)
    return out, dk0, dk1, dk2


def local(tokens, w_query, key_matrix, value_matrix, d_attended, doc_lengths):
    rows = tokens.shape[0]
    ctx = lax.axis_index("ctx").astype(jnp.int32)
    head = lax.axis_index("head").astype(jnp.int32)
    core, y = ctx % 2, (ctx // 2) % NY
    x, zh = head // NZH, head % NZH
    pos = jnp.stack([x, y, zh, 1 - 2 * core, core])

    feature = jnp.arange(tokens.shape[1], dtype=jnp.int32)
    target = feature // ROWS * PAD + feature % ROWS
    spread = (target[:, None] == jnp.arange(8 * PAD, dtype=jnp.int32)[None, :]).astype(BF)
    own = jnp.dot(tokens, spread, preferred_element_type=F32).astype(BF)

    partner = hop(own, dz=NZL)
    near = ring_x(own)
    far = ring_x(partner)

    w = gather_zcore(jnp.concatenate([key_matrix, value_matrix, w_query], axis=1))
    w = jnp.pad(w, ((0, 0), (0, PAD - ROWS), (0, 0)))
    kv_cols = 2 * HEAD_SIZE
    kv = ring_y(w[:, :, :kv_cols].reshape(NZL, PAIR, kv_cols), core)
    kv_a = hop(jnp.concatenate(kv[1:3], axis=0), swap=1)
    kv_b = hop(jnp.concatenate(kv[3:], axis=0), swap=1)
    qs = ring_y(w[:, :, kv_cols:].reshape(NZL, PAIR, -1), core)
    q_a = hop(jnp.concatenate(qs[1:], axis=0), swap=1)

    joined = project(pos, near, far, kv, [kv_a, kv_b], ((0, 0), (0, 4), (1, 0), (1, 4)), 1.0)
    query = project(pos, near, far, qs, [q_a], ((0, 0), (0, 4), (0, 8), (0, 12)), 0.0625)

    e2 = along_ctx(joined, 2)
    e1 = along_ctx(joined, 1)
    lead = (ctx * rows).reshape(1)
    attended, dk0, dk1, dk2 = attend(
        lead, doc_lengths.reshape(1, -1), query, joined, e1, e2, d_attended
    )
    key_total = dk0 + along_ctx(dk2, -2).astype(F32) + along_ctx(dk1, -1).astype(F32)
    return (attended, key_total.astype(BF))


def solution(mesh):
    return jax.shard_map(
        local,
        mesh=mesh,
        in_specs=(
            P("ctx", "head"),
            P("ctx", "head"),
            P("ctx", "head"),
            P("ctx", "head"),
            P("ctx", "head"),
            P(),
        ),
        out_specs=(P("ctx", "head"), P("ctx", "head")),
        check_vma=False,
    )
```

```python
import jax
import jax.numpy as jnp
from jax import lax
from jax.experimental import pallas as pl
from jax.experimental.pallas import tpu as pltpu
from jax.sharding import PartitionSpec as P


HEAD_SIZE = 256
WINDOW = 1024
NX, NY, NZL, NZH = 4, 8, 4, 2
NZ = NZL * NZH
ROWS = 60
PAD = 64
PAIR = 2 * PAD
BOTH = ("ctx", "head")
BF = jnp.bfloat16
F32 = jnp.float32
MIB = 1024 * 1024


def place(x, y, z, core):
    x, y, z = x % NX, y % NY, z % NZ
    ctx = (z % NZL) * 2 * NY + 2 * y + core
    return ctx * (NX * NZH) + x * NZH + z // NZL


def hop(block, dx=0, dy=0, dz=0, swap=0, by_core=False):
    route = []
    for x in range(NX):
        for y in range(NY):
            for z in range(NZ):
                for core in range(2):
                    s = 1 - 2 * core if by_core else 1
                    route.append(
                        (
                            place(x, y, z, core),
                            place(x + s * dx, y + s * dy, z + s * dz, core ^ swap),
                        )
                    )
    return lax.ppermute(block, BOTH, route)


def along_ctx(block, distance):
    n = lax.axis_size("ctx")
    route = [(i - distance, i) for i in range(n) if 0 <= i - distance < n]
    return lax.ppermute(block, "ctx", route)


def project_body(pos, t0, t1, t2, t3, p0, p1, p2, p3, own_ref, r1, r2, r3, r4, swapped, o_ref, *, scale):
    x, y, zh, sign = pos[0], pos[1], pos[2], pos[3]
    total = jnp.zeros(o_ref.shape, F32)

    for slot, (near, far) in enumerate(((t0, p0), (t1, p1), (t2, p2), (t3, p3))):
        z = lax.rem(x - sign * slot + NX, NX)

        def columns(distance):
            chip = lax.rem(y + sign * distance + NY, NY)
            at = pl.multiple_of(lax.rem(chip, 4) * PAIR, PAIR)
            return jnp.where(lax.div(chip, 4) == zh, near[:, pl.ds(at, PAIR)], far[:, pl.ds(at, PAIR)])

        left = [columns(d) for d in (0, 4, -1, 1, -2, 2, -3, 3)]
        right = [own_ref[z], r4[z]]
        for step, ref in enumerate((r1, r2, r3)):
            right += [ref[z], swapped[NZL * step + z]]
        total += jnp.dot(
            jnp.concatenate(left, axis=1),
            jnp.concatenate(right, axis=0),
            preferred_element_type=F32,
        )
    o_ref[...] = (total * scale).astype(BF)


def project(pos, near, far, ring, swapped, scale):
    rows = near[0].shape[0]
    cols = ring[0].shape[-1]
    full = pl.BlockSpec(memory_space=pltpu.VMEM)
    operands = [*near, *far, *ring, swapped]
    return pl.pallas_call(
        lambda *refs: project_body(*refs, scale=scale),
        out_shape=jax.ShapeDtypeStruct((rows, cols), BF),
        in_specs=[pl.BlockSpec(memory_space=pltpu.SMEM)] + [full] * len(operands),
        out_specs=full,
        cost_estimate=pl.CostEstimate(
            flops=2 * rows * 4096 * cols,
            bytes_accessed=2 * (rows * 4096 + cols * 4096 + rows * cols),
            transcendentals=0,
        ),
        compiler_params=pltpu.CompilerParams(vmem_limit_bytes=26 * MIB),
        name="project",
    )(pos, *operands)


def ring_y(block):
    out = [block]
    for _ in range(4):
        out.append(hop(out[-1], dy=1, by_core=True))
    return out


def ring_x(block):
    out = [block]
    for _ in range(3):
        out.append(hop(out[-1], dx=1, by_core=True))
    return out


def joined_blocks(blocks):
    return jnp.concatenate(blocks, axis=0)


def gather_zcore(w):
    groups = [
        [z * 2 * NY + 2 * y + core for z in range(NZL) for core in range(2)] for y in range(NY)
    ]
    return lax.all_gather(w, "ctx", axis=0, tiled=False, axis_index_groups=groups)


TILE = 256
REACH = 5 * TILE


def scores_body(lead, len_ref, q_ref, own, e1, e2, g_ref, p_ref, dk0, dk1, dk2, ext, s_ref, d_ref, acc):
    rows = q_ref.shape[0]
    ext[0:rows] = e2[...]
    ext[rows : 2 * rows] = e1[...]
    ext[2 * rows : 3 * rows] = own[...]
    acc[...] = jnp.zeros_like(acc)
    docs = len_ref.shape[1]
    i0 = lax.broadcasted_iota(jnp.int32, (docs, docs), 0)
    i1 = lax.broadcasted_iota(jnp.int32, (docs, docs), 1)
    starts = jnp.sum(jnp.where(i1 < i0, len_ref[...], 0), axis=1, keepdims=True)

    @pl.loop(0, 4)
    def _(step):
        i, h = lax.rem(step, 2), lax.div(step, 2)
        row0 = pl.multiple_of(i * TILE, TILE)
        col0 = pl.multiple_of(h * HEAD_SIZE, HEAD_SIZE)
        q = q_ref[pl.ds(row0, TILE), pl.ds(col0, HEAD_SIZE)]
        g = g_ref[pl.ds(row0, TILE), pl.ds(col0, HEAD_SIZE)]
        row = row0 + lax.broadcasted_iota(jnp.int32, (1, TILE), 1)
        at = lead[0] + row
        begin = jnp.max(jnp.where(starts <= at, starts, 0), axis=0, keepdims=True)
        low = jnp.maximum(begin - lead[0] + WINDOW, row + 1)
        nt = (((1,), (1,)), ((), ()))
        peak = jnp.full((1, TILE), -1e30, F32)
        for j in range(5):
            first = pl.multiple_of(row0 + j * TILE, TILE)
            s = lax.dot_general(ext[pl.ds(first, TILE), :HEAD_SIZE], q, nt, preferred_element_type=F32)
            key = first + lax.broadcasted_iota(jnp.int32, (TILE, 1), 0)
            ok = key >= low
            if j == 4:
                ok = ok & (key <= row + WINDOW)
            s = jnp.where(ok, s, -1e30)
            s_ref[j * TILE : (j + 1) * TILE] = s
            peak = jnp.maximum(peak, jnp.max(s, axis=0, keepdims=True))
        total = jnp.zeros((1, TILE), F32)
        for j in range(5):
            e = jnp.exp(s_ref[j * TILE : (j + 1) * TILE] - peak)
            s_ref[j * TILE : (j + 1) * TILE] = e
            total += jnp.sum(e, axis=0, keepdims=True)
        inverse = 1.0 / total
        delta = jnp.zeros((1, TILE), F32)
        for j in range(5):
            first = pl.multiple_of(row0 + j * TILE, TILE)
            d = lax.dot_general(ext[pl.ds(first, TILE), HEAD_SIZE:], g, nt, preferred_element_type=F32)
            p = s_ref[j * TILE : (j + 1) * TILE] * inverse
            s_ref[j * TILE : (j + 1) * TILE] = p
            d_ref[j * TILE : (j + 1) * TILE] = d
            p_ref[step, j * TILE : (j + 1) * TILE] = p.astype(BF)
            delta += jnp.sum(p * d, axis=0, keepdims=True)
        for j in range(5):
            first = pl.multiple_of(row0 + j * TILE, TILE)
            part = slice(j * TILE, (j + 1) * TILE)
            ds = (s_ref[part] * (d_ref[part] - delta)).astype(BF)
            acc[pl.ds(first, TILE)] += jnp.dot(ds, q, preferred_element_type=F32)

    dk2[...] = acc[0:rows].astype(BF)
    dk1[...] = acc[rows : 2 * rows].astype(BF)
    dk0[...] = acc[2 * rows : 3 * rows]


def values_body(p_ref, own, e1, e2, o_ref):
    tn = (((0,), (0,)), ((), ()))
    for i in range(2):
        value = jnp.concatenate(
            [e2[i * TILE :, HEAD_SIZE:], e1[:, HEAD_SIZE:], own[: (i + 1) * TILE, HEAD_SIZE:]], axis=0
        )
        for h in range(2):
            a = lax.dot_general(p_ref[2 * h + i], value, tn, preferred_element_type=F32)
            o_ref[i * TILE : (i + 1) * TILE, h * HEAD_SIZE : (h + 1) * HEAD_SIZE] = a.astype(BF)


def attend(lead, lens, query, own, e1, e2, grad):
    rows = query.shape[0]
    full = pl.BlockSpec(memory_space=pltpu.VMEM)
    smem = pl.BlockSpec(memory_space=pltpu.SMEM)
    shape = jax.ShapeDtypeStruct
    pairs = 4 * TILE * REACH
    p, dk0, dk1, dk2 = pl.pallas_call(
        scores_body,
        out_shape=(
            shape((4, REACH, TILE), BF),
            shape((rows, HEAD_SIZE), F32),
            shape((rows, HEAD_SIZE), BF),
            shape((rows, HEAD_SIZE), BF),
        ),
        in_specs=[smem] + [full] * 6,
        out_specs=(full,) * 4,
        scratch_shapes=[
            pltpu.VMEM((3 * rows, 2 * HEAD_SIZE), BF),
            pltpu.VMEM((REACH, TILE), F32),
            pltpu.VMEM((REACH, TILE), F32),
            pltpu.VMEM((3 * rows, HEAD_SIZE), F32),
        ],
        cost_estimate=pl.CostEstimate(
            flops=6 * pairs * HEAD_SIZE, bytes_accessed=5 * rows * 1024 + 2 * pairs, transcendentals=pairs
        ),
        compiler_params=pltpu.CompilerParams(vmem_limit_bytes=16 * MIB),
        name="scores",
    )(lead, lens, query, own, e1, e2, grad)
    out = pl.pallas_call(
        values_body,
        out_shape=shape((rows, 2 * HEAD_SIZE), BF),
        in_specs=[full] * 4,
        out_specs=full,
        cost_estimate=pl.CostEstimate(
            flops=2 * pairs * HEAD_SIZE, bytes_accessed=4 * rows * 1024 + 2 * pairs, transcendentals=0
        ),
        compiler_params=pltpu.CompilerParams(vmem_limit_bytes=14 * MIB),
        name="values",
    )(p, own, e1, e2)
    return out, dk0, dk1, dk2


def local(tokens, w_query, key_matrix, value_matrix, d_attended, doc_lengths):
    rows = tokens.shape[0]
    ctx = lax.axis_index("ctx").astype(jnp.int32)
    head = lax.axis_index("head").astype(jnp.int32)
    core, y = ctx % 2, (ctx // 2) % NY
    x, zh = head // NZH, head % NZH
    pos = jnp.stack([x, y, zh, 1 - 2 * core])

    feature = jnp.arange(tokens.shape[1], dtype=jnp.int32)
    target = feature // ROWS * PAD + feature % ROWS
    spread = (target[:, None] == jnp.arange(8 * PAD, dtype=jnp.int32)[None, :]).astype(BF)
    own = jnp.dot(tokens, spread, preferred_element_type=F32).astype(BF)

    partner = hop(own, dz=NZL)
    near = ring_x(own)
    far = [partner] + [hop(partner, dx=d, by_core=True) for d in (1, 2, 3)]

    w = gather_zcore(jnp.concatenate([key_matrix, value_matrix, w_query], axis=1))
    w = jnp.pad(w, ((0, 0), (0, PAD - ROWS), (0, 0)))
    kv_cols = 2 * HEAD_SIZE
    kv = ring_y(w[:, :, :kv_cols].reshape(NZL, PAIR, kv_cols))
    kv_a = hop(joined_blocks(kv[1:4]), swap=1)
    qs = ring_y(w[:, :, kv_cols:].reshape(NZL, PAIR, -1))
    q_a = hop(joined_blocks(qs[1:4]), swap=1)

    joined = project(pos, near, far, kv, kv_a, 1.0)
    query = project(pos, near, far, qs, q_a, 0.0625)

    e2 = along_ctx(joined, 2)
    e1 = along_ctx(joined, 1)
    lead = (ctx * rows).reshape(1)
    attended, dk0, dk1, dk2 = attend(
        lead, doc_lengths.reshape(1, -1), query, joined, e1, e2, d_attended
    )
    key_total = dk0 + along_ctx(dk2, -2).astype(F32) + along_ctx(dk1, -1).astype(F32)
    return (attended, key_total.astype(BF))


def solution(mesh):
    return jax.shard_map(
        local,
        mesh=mesh,
        in_specs=(
            P("ctx", "head"),
            P("ctx", "head"),
            P("ctx", "head"),
            P("ctx", "head"),
            P("ctx", "head"),
            P(),
        ),
        out_specs=(P("ctx", "head"), P("ctx", "head")),
        check_vma=False,
    )
```

```python
import jax
import jax.numpy as jnp
from jax import lax
from jax.experimental import pallas as pl
from jax.experimental.pallas import tpu as pltpu
from jax.sharding import PartitionSpec as P


HEAD_SIZE = 256
WINDOW = 1024
NX, NY, NZL, NZH = 4, 8, 4, 2
NZ = NZL * NZH
ROWS = 60
PAD = 64
PAIR = 2 * PAD
BOTH = ("ctx", "head")
BF = jnp.bfloat16
F32 = jnp.float32
MIB = 1024 * 1024


def place(x, y, z, core):
    x, y, z = x % NX, y % NY, z % NZ
    ctx = (z % NZL) * 2 * NY + 2 * y + core
    return ctx * (NX * NZH) + x * NZH + z // NZL


def hop(block, dx=0, dy=0, dz=0, swap=0, by_core=False):
    route = []
    for x in range(NX):
        for y in range(NY):
            for z in range(NZ):
                for core in range(2):
                    s = 1 - 2 * core if by_core else 1
                    route.append(
                        (
                            place(x, y, z, core),
                            place(x + s * dx, y + s * dy, z + s * dz, core ^ swap),
                        )
                    )
    return lax.ppermute(block, BOTH, route)


def along_ctx(block, distance):
    n = lax.axis_size("ctx")
    route = [(i - distance, i) for i in range(n) if 0 <= i - distance < n]
    return lax.ppermute(block, "ctx", route)


def project_body(t0, t1, t2, t3, p0, p1, p2, p3, own_ref, r1, r2, r3, r4, swapped, o_ref, *, scale):
    ctx = lax.axis_index("ctx").astype(jnp.int32)
    head = lax.axis_index("head").astype(jnp.int32)
    y = lax.rem(lax.div(ctx, 2), NY)
    sign = 1 - 2 * lax.rem(ctx, 2)
    x, zh = lax.div(head, NZH), lax.rem(head, NZH)
    total = jnp.zeros(o_ref.shape, F32)

    for slot, (near, far) in enumerate(((t0, p0), (t1, p1), (t2, p2), (t3, p3))):
        z = lax.rem(x - sign * slot + NX, NX)

        def columns(distance):
            chip = lax.rem(y + sign * distance + NY, NY)
            at = pl.multiple_of(lax.rem(chip, 4) * PAIR, PAIR)
            return jnp.where(lax.div(chip, 4) == zh, near[:, pl.ds(at, PAIR)], far[:, pl.ds(at, PAIR)])

        left = [columns(d) for d in (0, 4, -1, 1, -2, 2, -3, 3)]
        right = [own_ref[z], r4[z]]
        for step, ref in enumerate((r1, r2, r3)):
            right += [ref[z], swapped[NZL * step + z]]
        total += jnp.dot(
            jnp.concatenate(left, axis=1),
            jnp.concatenate(right, axis=0),
            preferred_element_type=F32,
        )
    o_ref[...] = (total * scale).astype(BF)


def project(near, far, ring, swapped, scale):
    rows = near[0].shape[0]
    cols = ring[0].shape[-1]
    full = pl.BlockSpec(memory_space=pltpu.VMEM)
    operands = [*near, *far, *ring, swapped]
    return pl.pallas_call(
        lambda *refs: project_body(*refs, scale=scale),
        out_shape=jax.ShapeDtypeStruct((rows, cols), BF),
        in_specs=[full] * len(operands),
        out_specs=full,
        cost_estimate=pl.CostEstimate(
            flops=2 * rows * 4096 * cols,
            bytes_accessed=2 * (rows * 4096 + cols * 4096 + rows * cols),
            transcendentals=0,
        ),
        compiler_params=pltpu.CompilerParams(vmem_limit_bytes=20 * MIB),
        name="project",
    )(*operands)


def ring_y(block):
    out = [block]
    for _ in range(4):
        out.append(hop(out[-1], dy=1, by_core=True))
    return out


def ring_x(block):
    out = [block]
    for _ in range(3):
        out.append(hop(out[-1], dx=1, by_core=True))
    return out


def join_body(*refs):
    *parts, o_ref = refs
    for i, part in enumerate(parts):
        o_ref[i * NZL : (i + 1) * NZL] = part[...]


def joined_blocks(blocks):
    full = pl.BlockSpec(memory_space=pltpu.VMEM)
    shape = (len(blocks) * NZL,) + blocks[0].shape[1:]
    return pl.pallas_call(
        join_body,
        out_shape=jax.ShapeDtypeStruct(shape, BF),
        in_specs=[full] * len(blocks),
        out_specs=full,
        cost_estimate=pl.CostEstimate(flops=0, bytes_accessed=4 * 2**20, transcendentals=0),
        compiler_params=pltpu.CompilerParams(vmem_limit_bytes=8 * MIB),
        name="join",
    )(*blocks)


def gather_zcore(w):
    groups = [
        [z * 2 * NY + 2 * y + core for z in range(NZL) for core in range(2)] for y in range(NY)
    ]
    return lax.all_gather(w, "ctx", axis=0, tiled=False, axis_index_groups=groups)


TILE = 256
REACH = 5 * TILE


def scores_body(len_ref, q_ref, own, e1, e2, g_ref, p_ref, dk0, dk1, dk2, ext, s_ref, d_ref, acc):
    rows = q_ref.shape[0]
    ext[0:rows] = e2[...]
    ext[rows : 2 * rows] = e1[...]
    ext[2 * rows : 3 * rows] = own[...]
    acc[...] = jnp.zeros_like(acc)
    docs = len_ref.shape[1]
    lead = lax.axis_index("ctx").astype(jnp.int32) * rows
    i0 = lax.broadcasted_iota(jnp.int32, (docs, docs), 0)
    i1 = lax.broadcasted_iota(jnp.int32, (docs, docs), 1)
    starts = jnp.sum(jnp.where(i1 < i0, len_ref[...], 0), axis=1, keepdims=True)

    @pl.loop(0, 4)
    def _(step):
        i, h = lax.rem(step, 2), lax.div(step, 2)
        row0 = pl.multiple_of(i * TILE, TILE)
        col0 = pl.multiple_of(h * HEAD_SIZE, HEAD_SIZE)
        q = q_ref[pl.ds(row0, TILE), pl.ds(col0, HEAD_SIZE)]
        g = g_ref[pl.ds(row0, TILE), pl.ds(col0, HEAD_SIZE)]
        row = row0 + lax.broadcasted_iota(jnp.int32, (1, TILE), 1)
        at = lead + row
        begin = jnp.max(jnp.where(starts <= at, starts, 0), axis=0, keepdims=True)
        low = jnp.maximum(begin - lead + WINDOW, row + 1)
        nt = (((1,), (1,)), ((), ()))
        peak = jnp.full((1, TILE), -1e30, F32)
        for j in range(5):
            first = pl.multiple_of(row0 + j * TILE, TILE)
            s = lax.dot_general(ext[pl.ds(first, TILE), :HEAD_SIZE], q, nt, preferred_element_type=F32)
            key = first + lax.broadcasted_iota(jnp.int32, (TILE, 1), 0)
            ok = key >= low
            if j == 4:
                ok = ok & (key <= row + WINDOW)
            s = jnp.where(ok, s, -1e30)
            s_ref[j * TILE : (j + 1) * TILE] = s
            peak = jnp.maximum(peak, jnp.max(s, axis=0, keepdims=True))
        total = jnp.zeros((1, TILE), F32)
        for j in range(5):
            e = jnp.exp(s_ref[j * TILE : (j + 1) * TILE] - peak)
            s_ref[j * TILE : (j + 1) * TILE] = e
            total += jnp.sum(e, axis=0, keepdims=True)
        inverse = 1.0 / total
        delta = jnp.zeros((1, TILE), F32)
        for j in range(5):
            first = pl.multiple_of(row0 + j * TILE, TILE)
            d = lax.dot_general(ext[pl.ds(first, TILE), HEAD_SIZE:], g, nt, preferred_element_type=F32)
            p = s_ref[j * TILE : (j + 1) * TILE] * inverse
            s_ref[j * TILE : (j + 1) * TILE] = p
            d_ref[j * TILE : (j + 1) * TILE] = d
            p_ref[step, j * TILE : (j + 1) * TILE] = p.astype(BF)
            delta += jnp.sum(p * d, axis=0, keepdims=True)
        for j in range(5):
            first = pl.multiple_of(row0 + j * TILE, TILE)
            part = slice(j * TILE, (j + 1) * TILE)
            ds = (s_ref[part] * (d_ref[part] - delta)).astype(BF)
            acc[pl.ds(first, TILE)] += jnp.dot(ds, q, preferred_element_type=F32)

    dk2[...] = acc[0:rows].astype(BF)
    dk1[...] = acc[rows : 2 * rows].astype(BF)
    dk0[...] = acc[2 * rows : 3 * rows]


def values_body(p_ref, own, e1, e2, o_ref):
    tn = (((0,), (0,)), ((), ()))
    for i in range(2):
        value = jnp.concatenate(
            [e2[i * TILE :, HEAD_SIZE:], e1[:, HEAD_SIZE:], own[: (i + 1) * TILE, HEAD_SIZE:]], axis=0
        )
        for h in range(2):
            a = lax.dot_general(p_ref[2 * h + i], value, tn, preferred_element_type=F32)
            o_ref[i * TILE : (i + 1) * TILE, h * HEAD_SIZE : (h + 1) * HEAD_SIZE] = a.astype(BF)


def attend(lens, query, own, e1, e2, grad):
    rows = query.shape[0]
    full = pl.BlockSpec(memory_space=pltpu.VMEM)
    shape = jax.ShapeDtypeStruct
    pairs = 4 * TILE * REACH
    p, dk0, dk1, dk2 = pl.pallas_call(
        scores_body,
        out_shape=(
            shape((4, REACH, TILE), BF),
            shape((rows, HEAD_SIZE), F32),
            shape((rows, HEAD_SIZE), BF),
            shape((rows, HEAD_SIZE), BF),
        ),
        in_specs=[full] * 6,
        out_specs=(full,) * 4,
        scratch_shapes=[
            pltpu.VMEM((3 * rows, 2 * HEAD_SIZE), BF),
            pltpu.VMEM((REACH, TILE), F32),
            pltpu.VMEM((REACH, TILE), F32),
            pltpu.VMEM((3 * rows, HEAD_SIZE), F32),
        ],
        cost_estimate=pl.CostEstimate(
            flops=6 * pairs * HEAD_SIZE, bytes_accessed=5 * rows * 1024 + 2 * pairs, transcendentals=pairs
        ),
        compiler_params=pltpu.CompilerParams(vmem_limit_bytes=16 * MIB),
        name="scores",
    )(lens, query, own, e1, e2, grad)
    out = pl.pallas_call(
        values_body,
        out_shape=shape((rows, 2 * HEAD_SIZE), BF),
        in_specs=[full] * 4,
        out_specs=full,
        cost_estimate=pl.CostEstimate(
            flops=2 * pairs * HEAD_SIZE, bytes_accessed=4 * rows * 1024 + 2 * pairs, transcendentals=0
        ),
        compiler_params=pltpu.CompilerParams(vmem_limit_bytes=14 * MIB),
        name="values",
    )(p, own, e1, e2)
    return out, dk0, dk1, dk2


def local(tokens, w_query, key_matrix, value_matrix, d_attended, doc_lengths):
    feature = jnp.arange(tokens.shape[1], dtype=jnp.int32)
    target = feature // ROWS * PAD + feature % ROWS
    spread = (target[:, None] == jnp.arange(8 * PAD, dtype=jnp.int32)[None, :]).astype(BF)
    own = jnp.dot(tokens, spread, preferred_element_type=F32).astype(BF)

    partner = hop(own, dz=NZL)
    near = ring_x(own)
    far = [partner] + [hop(partner, dx=d, by_core=True) for d in (1, 2, 3)]

    w = gather_zcore(jnp.concatenate([key_matrix, value_matrix, w_query], axis=1))
    w = jnp.pad(w, ((0, 0), (0, PAD - ROWS), (0, 0)))
    kv_cols = 2 * HEAD_SIZE
    kv = ring_y(w[:, :, :kv_cols].reshape(NZL, PAIR, kv_cols))
    kv_a = hop(joined_blocks(kv[1:4]), swap=1)
    qs = ring_y(w[:, :, kv_cols:].reshape(NZL, PAIR, -1))
    q_a = hop(joined_blocks(qs[1:4]), swap=1)

    joined = project(near, far, kv, kv_a, 1.0)
    query = project(near, far, qs, q_a, 0.0625)

    e2 = along_ctx(joined, 2)
    e1 = along_ctx(joined, 1)
    attended, dk0, dk1, dk2 = attend(
        doc_lengths.reshape(1, -1), query, joined, e1, e2, d_attended
    )
    key_total = dk0 + along_ctx(dk2, -2).astype(F32) + along_ctx(dk1, -1).astype(F32)
    return (attended, key_total.astype(BF))


def solution(mesh):
    return jax.shard_map(
        local,
        mesh=mesh,
        in_specs=(
            P("ctx", "head"),
            P("ctx", "head"),
            P("ctx", "head"),
            P("ctx", "head"),
            P("ctx", "head"),
            P(),
        ),
        out_specs=(P("ctx", "head"), P("ctx", "head")),
        check_vma=False,
    )
```

```python
import jax
import jax.numpy as jnp
from jax import lax
from jax.experimental import pallas as pl
from jax.experimental.pallas import tpu as pltpu
from jax.sharding import PartitionSpec as P


HEAD_SIZE = 256
WINDOW = 1024
NX, NY, NZL, NZH = 4, 8, 4, 2
NZ = NZL * NZH
ROWS = 60
PAD = 64
PAIR = 2 * PAD
BOTH = ("ctx", "head")
BF = jnp.bfloat16
F32 = jnp.float32
MIB = 1024 * 1024


def place(x, y, z, core):
    x, y, z = x % NX, y % NY, z % NZ
    ctx = (z % NZL) * 2 * NY + 2 * y + core
    return ctx * (NX * NZH) + x * NZH + z // NZL


def hop(block, dx=0, dy=0, dz=0, swap=0, by_core=False):
    route = []
    for x in range(NX):
        for y in range(NY):
            for z in range(NZ):
                for core in range(2):
                    s = 1 - 2 * core if by_core else 1
                    route.append(
                        (
                            place(x, y, z, core),
                            place(x + s * dx, y + s * dy, z + s * dz, core ^ swap),
                        )
                    )
    return lax.ppermute(block, BOTH, route)


def along_ctx(block, distance):
    n = lax.axis_size("ctx")
    route = [(i - distance, i) for i in range(n) if 0 <= i - distance < n]
    return lax.ppermute(block, "ctx", route)


def project_body(t0, t1, t2, t3, p0, p1, p2, p3, own_ref, r1, r2, r3, r4, swapped, o_ref, *, scale):
    ctx = lax.axis_index("ctx").astype(jnp.int32)
    head = lax.axis_index("head").astype(jnp.int32)
    y = lax.rem(lax.div(ctx, 2), NY)
    sign = 1 - 2 * lax.rem(ctx, 2)
    x, zh = lax.div(head, NZH), lax.rem(head, NZH)
    total = jnp.zeros(o_ref.shape, F32)

    for slot, (near, far) in enumerate(((t0, p0), (t1, p1), (t2, p2), (t3, p3))):
        z = lax.rem(x - sign * slot + NX, NX)

        def columns(distance):
            chip = lax.rem(y + sign * distance + NY, NY)
            at = pl.multiple_of(lax.rem(chip, 4) * PAIR, PAIR)
            return jnp.where(lax.div(chip, 4) == zh, near[:, pl.ds(at, PAIR)], far[:, pl.ds(at, PAIR)])

        left = [columns(d) for d in (0, 4, -1, 1, -2, 2, -3, 3)]
        right = [own_ref[z], r4[z]]
        for step, ref in enumerate((r1, r2, r3)):
            right += [ref[z], swapped[NZL * step + z]]
        total += jnp.dot(
            jnp.concatenate(left, axis=1),
            jnp.concatenate(right, axis=0),
            preferred_element_type=F32,
        )
    o_ref[...] = (total * scale).astype(BF)


def project(near, far, ring, swapped, scale):
    rows = near[0].shape[0]
    cols = ring[0].shape[-1]
    full = pl.BlockSpec(memory_space=pltpu.VMEM)
    operands = [*near, *far, *ring, swapped]
    return pl.pallas_call(
        lambda *refs: project_body(*refs, scale=scale),
        out_shape=jax.ShapeDtypeStruct((rows, cols), BF),
        in_specs=[full] * len(operands),
        out_specs=full,
        cost_estimate=pl.CostEstimate(
            flops=2 * rows * 4096 * cols,
            bytes_accessed=2 * (rows * 4096 + cols * 4096 + rows * cols),
            transcendentals=0,
        ),
        compiler_params=pltpu.CompilerParams(vmem_limit_bytes=20 * MIB),
        name="project",
    )(*operands)


def ring_y(block):
    out = [block]
    for _ in range(4):
        out.append(hop(out[-1], dy=1, by_core=True))
    return out


def ring_x(block):
    one = hop(block, dx=1, by_core=True)
    three = hop(block, dx=3, by_core=True)
    two = hop(one, dx=1, by_core=True)
    return [block, one, two, three]


def join_body(*refs):
    *parts, o_ref = refs
    for i, part in enumerate(parts):
        o_ref[i * NZL : (i + 1) * NZL] = part[...]


def joined_blocks(blocks):
    full = pl.BlockSpec(memory_space=pltpu.VMEM)
    shape = (len(blocks) * NZL,) + blocks[0].shape[1:]
    return pl.pallas_call(
        join_body,
        out_shape=jax.ShapeDtypeStruct(shape, BF),
        in_specs=[full] * len(blocks),
        out_specs=full,
        cost_estimate=pl.CostEstimate(flops=0, bytes_accessed=4 * 2**20, transcendentals=0),
        compiler_params=pltpu.CompilerParams(vmem_limit_bytes=8 * MIB),
        name="join",
    )(*blocks)


def gather_zcore(w):
    groups = [
        [z * 2 * NY + 2 * y + core for z in range(NZL) for core in range(2)] for y in range(NY)
    ]
    return lax.all_gather(w, "ctx", axis=0, tiled=False, axis_index_groups=groups)


TILE = 256
REACH = 5 * TILE


def scores_body(len_ref, q_ref, own, e1, e2, g_ref, p_ref, dk0, dk1, dk2, ext, s_ref, d_ref, acc):
    rows = q_ref.shape[0]
    ext[0:rows] = e2[...]
    ext[rows : 2 * rows] = e1[...]
    ext[2 * rows : 3 * rows] = own[...]
    acc[...] = jnp.zeros_like(acc)
    docs = len_ref.shape[1]
    lead = lax.axis_index("ctx").astype(jnp.int32) * rows
    i0 = lax.broadcasted_iota(jnp.int32, (docs, docs), 0)
    i1 = lax.broadcasted_iota(jnp.int32, (docs, docs), 1)
    starts = jnp.sum(jnp.where(i1 < i0, len_ref[...], 0), axis=1, keepdims=True)

    @pl.loop(0, 4)
    def _(step):
        i, h = lax.rem(step, 2), lax.div(step, 2)
        row0 = pl.multiple_of(i * TILE, TILE)
        col0 = pl.multiple_of(h * HEAD_SIZE, HEAD_SIZE)
        q = q_ref[pl.ds(row0, TILE), pl.ds(col0, HEAD_SIZE)]
        g = g_ref[pl.ds(row0, TILE), pl.ds(col0, HEAD_SIZE)]
        row = row0 + lax.broadcasted_iota(jnp.int32, (1, TILE), 1)
        at = lead + row
        begin = jnp.max(jnp.where(starts <= at, starts, 0), axis=0, keepdims=True)
        low = jnp.maximum(begin - lead + WINDOW, row + 1)
        nt = (((1,), (1,)), ((), ()))
        peak = jnp.full((1, TILE), -1e30, F32)
        for j in range(5):
            first = pl.multiple_of(row0 + j * TILE, TILE)
            s = lax.dot_general(ext[pl.ds(first, TILE), :HEAD_SIZE], q, nt, preferred_element_type=F32)
            key = first + lax.broadcasted_iota(jnp.int32, (TILE, 1), 0)
            ok = key >= low
            if j == 4:
                ok = ok & (key <= row + WINDOW)
            s = jnp.where(ok, s, -1e30)
            s_ref[j * TILE : (j + 1) * TILE] = s
            peak = jnp.maximum(peak, jnp.max(s, axis=0, keepdims=True))
        total = jnp.zeros((1, TILE), F32)
        for j in range(5):
            e = jnp.exp(s_ref[j * TILE : (j + 1) * TILE] - peak)
            s_ref[j * TILE : (j + 1) * TILE] = e
            total += jnp.sum(e, axis=0, keepdims=True)
        inverse = 1.0 / total
        delta = jnp.zeros((1, TILE), F32)
        for j in range(5):
            first = pl.multiple_of(row0 + j * TILE, TILE)
            d = lax.dot_general(ext[pl.ds(first, TILE), HEAD_SIZE:], g, nt, preferred_element_type=F32)
            p = s_ref[j * TILE : (j + 1) * TILE] * inverse
            s_ref[j * TILE : (j + 1) * TILE] = p
            d_ref[j * TILE : (j + 1) * TILE] = d
            p_ref[step, j * TILE : (j + 1) * TILE] = p.astype(BF)
            delta += jnp.sum(p * d, axis=0, keepdims=True)
        for j in range(5):
            first = pl.multiple_of(row0 + j * TILE, TILE)
            part = slice(j * TILE, (j + 1) * TILE)
            ds = (s_ref[part] * (d_ref[part] - delta)).astype(BF)
            acc[pl.ds(first, TILE)] += jnp.dot(ds, q, preferred_element_type=F32)

    dk2[...] = acc[0:rows].astype(BF)
    dk1[...] = acc[rows : 2 * rows].astype(BF)
    dk0[...] = acc[2 * rows : 3 * rows]


def values_body(p_ref, own, e1, e2, o_ref):
    tn = (((0,), (0,)), ((), ()))
    for i in range(2):
        value = jnp.concatenate(
            [e2[i * TILE :, HEAD_SIZE:], e1[:, HEAD_SIZE:], own[: (i + 1) * TILE, HEAD_SIZE:]], axis=0
        )
        for h in range(2):
            a = lax.dot_general(p_ref[2 * h + i], value, tn, preferred_element_type=F32)
            o_ref[i * TILE : (i + 1) * TILE, h * HEAD_SIZE : (h + 1) * HEAD_SIZE] = a.astype(BF)


def attend(lens, query, own, e1, e2, grad):
    rows = query.shape[0]
    full = pl.BlockSpec(memory_space=pltpu.VMEM)
    shape = jax.ShapeDtypeStruct
    pairs = 4 * TILE * REACH
    p, dk0, dk1, dk2 = pl.pallas_call(
        scores_body,
        out_shape=(
            shape((4, REACH, TILE), BF),
            shape((rows, HEAD_SIZE), F32),
            shape((rows, HEAD_SIZE), BF),
            shape((rows, HEAD_SIZE), BF),
        ),
        in_specs=[full] * 6,
        out_specs=(full,) * 4,
        scratch_shapes=[
            pltpu.VMEM((3 * rows, 2 * HEAD_SIZE), BF),
            pltpu.VMEM((REACH, TILE), F32),
            pltpu.VMEM((REACH, TILE), F32),
            pltpu.VMEM((3 * rows, HEAD_SIZE), F32),
        ],
        cost_estimate=pl.CostEstimate(
            flops=6 * pairs * HEAD_SIZE, bytes_accessed=5 * rows * 1024 + 2 * pairs, transcendentals=pairs
        ),
        compiler_params=pltpu.CompilerParams(vmem_limit_bytes=16 * MIB),
        name="scores",
    )(lens, query, own, e1, e2, grad)
    out = pl.pallas_call(
        values_body,
        out_shape=shape((rows, 2 * HEAD_SIZE), BF),
        in_specs=[full] * 4,
        out_specs=full,
        cost_estimate=pl.CostEstimate(
            flops=2 * pairs * HEAD_SIZE, bytes_accessed=4 * rows * 1024 + 2 * pairs, transcendentals=0
        ),
        compiler_params=pltpu.CompilerParams(vmem_limit_bytes=14 * MIB),
        name="values",
    )(p, own, e1, e2)
    return out, dk0, dk1, dk2


def local(tokens, w_query, key_matrix, value_matrix, d_attended, doc_lengths):
    feature = jnp.arange(tokens.shape[1], dtype=jnp.int32)
    target = feature // ROWS * PAD + feature % ROWS
    spread = (target[:, None] == jnp.arange(8 * PAD, dtype=jnp.int32)[None, :]).astype(BF)
    own = jnp.dot(tokens, spread, preferred_element_type=F32).astype(BF)

    partner = hop(own, dz=NZL)
    near = ring_x(own)
    far = ring_x(partner)

    w = gather_zcore(jnp.concatenate([key_matrix, value_matrix, w_query], axis=1))
    w = jnp.pad(w, ((0, 0), (0, PAD - ROWS), (0, 0)))
    kv_cols = 2 * HEAD_SIZE
    kv = ring_y(w[:, :, :kv_cols].reshape(NZL, PAIR, kv_cols))
    kv_a = hop(joined_blocks(kv[1:4]), swap=1)
    qs = ring_y(w[:, :, kv_cols:].reshape(NZL, PAIR, -1))
    q_a = hop(joined_blocks(qs[1:4]), swap=1)

    joined = project(near, far, kv, kv_a, 1.0)
    query = project(near, far, qs, q_a, 0.0625)

    e2 = along_ctx(joined, 2)
    e1 = along_ctx(joined, 1)
    attended, dk0, dk1, dk2 = attend(
        doc_lengths.reshape(1, -1), query, joined, e1, e2, d_attended
    )
    key_total = dk0 + along_ctx(dk2, -2).astype(F32) + along_ctx(dk1, -1).astype(F32)
    return (attended, key_total.astype(BF))


def solution(mesh):
    return jax.shard_map(
        local,
        mesh=mesh,
        in_specs=(
            P("ctx", "head"),
            P("ctx", "head"),
            P("ctx", "head"),
            P("ctx", "head"),
            P("ctx", "head"),
            P(),
        ),
        out_specs=(P("ctx", "head"), P("ctx", "head")),
        check_vma=False,
    )
```

```python
import jax
import jax.numpy as jnp
from jax import lax
from jax.experimental import pallas as pl
from jax.experimental.pallas import tpu as pltpu
from jax.sharding import PartitionSpec as P


HEAD_SIZE = 256
WINDOW = 1024
NX, NY, NZL, NZH = 4, 8, 4, 2
NZ = NZL * NZH
ROWS = 60
PAD = 64
PAIR = 2 * PAD
BOTH = ("ctx", "head")
BF = jnp.bfloat16
F32 = jnp.float32
MIB = 1024 * 1024


def place(x, y, z, core):
    x, y, z = x % NX, y % NY, z % NZ
    ctx = (z % NZL) * 2 * NY + 2 * y + core
    return ctx * (NX * NZH) + x * NZH + z // NZL


def hop(block, dx=0, dy=0, dz=0, swap=0, by_core=False):
    route = []
    for x in range(NX):
        for y in range(NY):
            for z in range(NZ):
                for core in range(2):
                    s = 1 - 2 * core if by_core else 1
                    route.append(
                        (
                            place(x, y, z, core),
                            place(x + s * dx, y + s * dy, z + s * dz, core ^ swap),
                        )
                    )
    return lax.ppermute(block, BOTH, route)


def along_ctx(block, distance):
    n = lax.axis_size("ctx")
    route = [(i - distance, i) for i in range(n) if 0 <= i - distance < n]
    return lax.ppermute(block, "ctx", route)


def project_body(t0, t1, t2, t3, p0, p1, p2, p3, own_ref, r1, r2, r3, r4, swapped, o_ref, *, scale):
    ctx = lax.axis_index("ctx").astype(jnp.int32)
    head = lax.axis_index("head").astype(jnp.int32)
    y = lax.rem(lax.div(ctx, 2), NY)
    sign = 1 - 2 * lax.rem(ctx, 2)
    x, zh = lax.div(head, NZH), lax.rem(head, NZH)
    total = jnp.zeros(o_ref.shape, F32)

    for slot, (near, far) in enumerate(((t0, p0), (t1, p1), (t2, p2), (t3, p3))):
        z = lax.rem(x - sign * slot + NX, NX)

        def columns(distance):
            chip = lax.rem(y + sign * distance + NY, NY)
            at = pl.multiple_of(lax.rem(chip, 4) * PAIR, PAIR)
            return jnp.where(lax.div(chip, 4) == zh, near[:, pl.ds(at, PAIR)], far[:, pl.ds(at, PAIR)])

        left = [columns(d) for d in (0, 4, -1, 1, -2, 2, -3, 3)]
        right = [own_ref[z], own_ref[NZL + z], r4[z], r4[NZL + z]]
        for step, ref in enumerate((r1, r2, r3)):
            at = 2 * NZL * step + z
            right += [ref[z], ref[NZL + z], swapped[at], swapped[at + NZL]]
        total += jnp.dot(
            jnp.concatenate(left, axis=1),
            jnp.concatenate(right, axis=0),
            preferred_element_type=F32,
        )
    o_ref[...] = (total * scale).astype(BF)


def project(near, far, ring, swapped, scale):
    rows = near[0].shape[0]
    cols = ring[0].shape[-1]
    full = pl.BlockSpec(memory_space=pltpu.VMEM)
    operands = [*near, *far, *ring, swapped]
    return pl.pallas_call(
        lambda *refs: project_body(*refs, scale=scale),
        out_shape=jax.ShapeDtypeStruct((rows, cols), BF),
        in_specs=[full] * len(operands),
        out_specs=full,
        cost_estimate=pl.CostEstimate(
            flops=2 * rows * 4096 * cols,
            bytes_accessed=2 * (rows * 4096 + cols * 4096 + rows * cols),
            transcendentals=0,
        ),
        compiler_params=pltpu.CompilerParams(vmem_limit_bytes=20 * MIB),
        name="project",
    )(*operands)


def ring_y(block):
    out = [block]
    for _ in range(4):
        out.append(hop(out[-1], dy=1, by_core=True))
    return out


def ring_x(block):
    one = hop(block, dx=1, by_core=True)
    three = hop(block, dx=3, by_core=True)
    two = hop(one, dx=1, by_core=True)
    return [block, one, two, three]


def join_body(*refs):
    *parts, o_ref = refs
    for i, part in enumerate(parts):
        o_ref[i * 2 * NZL : (i + 1) * 2 * NZL] = part[...]


def joined_blocks(blocks):
    full = pl.BlockSpec(memory_space=pltpu.VMEM)
    shape = (len(blocks) * 2 * NZL,) + blocks[0].shape[1:]
    return pl.pallas_call(
        join_body,
        out_shape=jax.ShapeDtypeStruct(shape, BF),
        in_specs=[full] * len(blocks),
        out_specs=full,
        cost_estimate=pl.CostEstimate(flops=0, bytes_accessed=4 * 2**20, transcendentals=0),
        compiler_params=pltpu.CompilerParams(vmem_limit_bytes=8 * MIB),
        name="join",
    )(*blocks)


def gather_zcore(w):
    def index(z, y, core):
        return z * 2 * NY + 2 * y + core

    lines = [[index(z, y, core) for z in range(NZL)] for y in range(NY) for core in range(2)]
    chips = [[index(z, y, core) for core in range(2)] for z in range(NZL) for y in range(NY)]
    w = lax.all_gather(w, "ctx", axis=0, tiled=False, axis_index_groups=lines)
    w = lax.all_gather(w, "ctx", axis=0, tiled=False, axis_index_groups=chips)
    return w.reshape((2 * NZL,) + w.shape[2:])


TILE = 256
REACH = 5 * TILE


def scores_body(len_ref, q_ref, own, e1, e2, g_ref, p_ref, dk0, dk1, dk2, ext, s_ref, d_ref, acc):
    rows = q_ref.shape[0]
    ext[0:rows] = e2[...]
    ext[rows : 2 * rows] = e1[...]
    ext[2 * rows : 3 * rows] = own[...]
    acc[...] = jnp.zeros_like(acc)
    docs = len_ref.shape[1]
    lead = lax.axis_index("ctx").astype(jnp.int32) * rows
    i0 = lax.broadcasted_iota(jnp.int32, (docs, docs), 0)
    i1 = lax.broadcasted_iota(jnp.int32, (docs, docs), 1)
    starts = jnp.sum(jnp.where(i1 < i0, len_ref[...], 0), axis=1, keepdims=True)

    @pl.loop(0, 4)
    def _(step):
        i, h = lax.rem(step, 2), lax.div(step, 2)
        row0 = pl.multiple_of(i * TILE, TILE)
        col0 = pl.multiple_of(h * HEAD_SIZE, HEAD_SIZE)
        q = q_ref[pl.ds(row0, TILE), pl.ds(col0, HEAD_SIZE)]
        g = g_ref[pl.ds(row0, TILE), pl.ds(col0, HEAD_SIZE)]
        row = row0 + lax.broadcasted_iota(jnp.int32, (1, TILE), 1)
        at = lead + row
        begin = jnp.max(jnp.where(starts <= at, starts, 0), axis=0, keepdims=True)
        low = jnp.maximum(begin - lead + WINDOW, row + 1)
        nt = (((1,), (1,)), ((), ()))
        peak = jnp.full((1, TILE), -1e30, F32)
        for j in range(5):
            first = pl.multiple_of(row0 + j * TILE, TILE)
            s = lax.dot_general(ext[pl.ds(first, TILE), :HEAD_SIZE], q, nt, preferred_element_type=F32)
            key = first + lax.broadcasted_iota(jnp.int32, (TILE, 1), 0)
            ok = key >= low
            if j == 4:
                ok = ok & (key <= row + WINDOW)
            s = jnp.where(ok, s, -1e30)
            s_ref[j * TILE : (j + 1) * TILE] = s
            peak = jnp.maximum(peak, jnp.max(s, axis=0, keepdims=True))
        total = jnp.zeros((1, TILE), F32)
        for j in range(5):
            e = jnp.exp(s_ref[j * TILE : (j + 1) * TILE] - peak)
            s_ref[j * TILE : (j + 1) * TILE] = e
            total += jnp.sum(e, axis=0, keepdims=True)
        inverse = 1.0 / total
        delta = jnp.zeros((1, TILE), F32)
        for j in range(5):
            first = pl.multiple_of(row0 + j * TILE, TILE)
            d = lax.dot_general(ext[pl.ds(first, TILE), HEAD_SIZE:], g, nt, preferred_element_type=F32)
            p = s_ref[j * TILE : (j + 1) * TILE] * inverse
            s_ref[j * TILE : (j + 1) * TILE] = p
            d_ref[j * TILE : (j + 1) * TILE] = d
            p_ref[step, j * TILE : (j + 1) * TILE] = p.astype(BF)
            delta += jnp.sum(p * d, axis=0, keepdims=True)
        for j in range(5):
            first = pl.multiple_of(row0 + j * TILE, TILE)
            part = slice(j * TILE, (j + 1) * TILE)
            ds = (s_ref[part] * (d_ref[part] - delta)).astype(BF)
            acc[pl.ds(first, TILE)] += jnp.dot(ds, q, preferred_element_type=F32)

    dk2[...] = acc[0:rows].astype(BF)
    dk1[...] = acc[rows : 2 * rows].astype(BF)
    dk0[...] = acc[2 * rows : 3 * rows]


def values_body(p_ref, own, e1, e2, o_ref):
    tn = (((0,), (0,)), ((), ()))
    for i in range(2):
        value = jnp.concatenate(
            [e2[i * TILE :, HEAD_SIZE:], e1[:, HEAD_SIZE:], own[: (i + 1) * TILE, HEAD_SIZE:]], axis=0
        )
        for h in range(2):
            a = lax.dot_general(p_ref[2 * h + i], value, tn, preferred_element_type=F32)
            o_ref[i * TILE : (i + 1) * TILE, h * HEAD_SIZE : (h + 1) * HEAD_SIZE] = a.astype(BF)


def attend(lens, query, own, e1, e2, grad):
    rows = query.shape[0]
    full = pl.BlockSpec(memory_space=pltpu.VMEM)
    shape = jax.ShapeDtypeStruct
    pairs = 4 * TILE * REACH
    p, dk0, dk1, dk2 = pl.pallas_call(
        scores_body,
        out_shape=(
            shape((4, REACH, TILE), BF),
            shape((rows, HEAD_SIZE), F32),
            shape((rows, HEAD_SIZE), BF),
            shape((rows, HEAD_SIZE), BF),
        ),
        in_specs=[full] * 6,
        out_specs=(full,) * 4,
        scratch_shapes=[
            pltpu.VMEM((3 * rows, 2 * HEAD_SIZE), BF),
            pltpu.VMEM((REACH, TILE), F32),
            pltpu.VMEM((REACH, TILE), F32),
            pltpu.VMEM((3 * rows, HEAD_SIZE), F32),
        ],
        cost_estimate=pl.CostEstimate(
            flops=6 * pairs * HEAD_SIZE, bytes_accessed=5 * rows * 1024 + 2 * pairs, transcendentals=pairs
        ),
        compiler_params=pltpu.CompilerParams(vmem_limit_bytes=16 * MIB),
        name="scores",
    )(lens, query, own, e1, e2, grad)
    out = pl.pallas_call(
        values_body,
        out_shape=shape((rows, 2 * HEAD_SIZE), BF),
        in_specs=[full] * 4,
        out_specs=full,
        cost_estimate=pl.CostEstimate(
            flops=2 * pairs * HEAD_SIZE, bytes_accessed=4 * rows * 1024 + 2 * pairs, transcendentals=0
        ),
        compiler_params=pltpu.CompilerParams(vmem_limit_bytes=14 * MIB),
        name="values",
    )(p, own, e1, e2)
    return out, dk0, dk1, dk2


def local(tokens, w_query, key_matrix, value_matrix, d_attended, doc_lengths):
    feature = jnp.arange(tokens.shape[1], dtype=jnp.int32)
    target = feature // ROWS * PAD + feature % ROWS
    spread = (target[:, None] == jnp.arange(8 * PAD, dtype=jnp.int32)[None, :]).astype(BF)
    own = jnp.dot(tokens, spread, preferred_element_type=F32).astype(BF)

    partner = hop(own, dz=NZL)
    near = ring_x(own)
    far = ring_x(partner)

    w = gather_zcore(jnp.concatenate([key_matrix, value_matrix, w_query], axis=1))
    w = jnp.pad(w, ((0, 0), (0, PAD - ROWS), (0, 0)))
    kv_cols = 2 * HEAD_SIZE
    kv = ring_y(w[..., :kv_cols])
    kv_a = hop(joined_blocks(kv[1:4]), swap=1)
    qs = ring_y(w[..., kv_cols:])
    q_a = hop(joined_blocks(qs[1:4]), swap=1)

    joined = project(near, far, kv, kv_a, 1.0)
    query = project(near, far, qs, q_a, 0.0625)

    e2 = along_ctx(joined, 2)
    e1 = along_ctx(joined, 1)
    attended, dk0, dk1, dk2 = attend(
        doc_lengths.reshape(1, -1), query, joined, e1, e2, d_attended
    )
    key_total = dk0 + along_ctx(dk2, -2).astype(F32) + along_ctx(dk1, -1).astype(F32)
    return (attended, key_total.astype(BF))


def solution(mesh):
    return jax.shard_map(
        local,
        mesh=mesh,
        in_specs=(
            P("ctx", "head"),
            P("ctx", "head"),
            P("ctx", "head"),
            P("ctx", "head"),
            P("ctx", "head"),
            P(),
        ),
        out_specs=(P("ctx", "head"), P("ctx", "head")),
        check_vma=False,
    )
```

```python
import jax
import jax.numpy as jnp
from jax import lax
from jax.experimental import pallas as pl
from jax.experimental.pallas import tpu as pltpu
from jax.sharding import PartitionSpec as P


HEAD_SIZE = 256
WINDOW = 1024
NX, NY, NZL, NZH = 4, 8, 4, 2
NZ = NZL * NZH
ROWS = 60
PAD = 64
PAIR = 2 * PAD
BOTH = ("ctx", "head")
BF = jnp.bfloat16
F32 = jnp.float32
MIB = 1024 * 1024


def place(x, y, z, core):
    x, y, z = x % NX, y % NY, z % NZ
    ctx = (z % NZL) * 2 * NY + 2 * y + core
    return ctx * (NX * NZH) + x * NZH + z // NZL


def hop(block, dx=0, dy=0, dz=0, swap=0, by_core=False, flip=0):
    route = []
    for x in range(NX):
        for y in range(NY):
            for z in range(NZ):
                for core in range(2):
                    s = 1 - 2 * core if by_core else 1
                    route.append(
                        (
                            place(x, y, z, core),
                            place(x + s * dx, y + s * dy, (z ^ flip) + s * dz, core ^ swap),
                        )
                    )
    return lax.ppermute(block, BOTH, route)


def along_ctx(block, distance):
    n = lax.axis_size("ctx")
    route = [(i - distance, i) for i in range(n) if 0 <= i - distance < n]
    return lax.ppermute(block, "ctx", route)


def project_body(t0, t1, t2, t3, p0, p1, p2, p3, own_ref, r1, r2, r3, r4, swapped, o_ref, *, scale):
    ctx = lax.axis_index("ctx").astype(jnp.int32)
    head = lax.axis_index("head").astype(jnp.int32)
    y = lax.rem(lax.div(ctx, 2), NY)
    own_z = lax.div(ctx, 2 * NY)
    sign = 1 - 2 * lax.rem(ctx, 2)
    x, zh = lax.div(head, NZH), lax.rem(head, NZH)
    total = jnp.zeros(o_ref.shape, F32)

    for slot, (near, far) in enumerate(((t0, p0), (t1, p1), (t2, p2), (t3, p3))):
        z = lax.rem(x - sign * slot + NX, NX)

        def columns(distance):
            chip = lax.rem(y + sign * distance + NY, NY)
            at = pl.multiple_of(lax.rem(chip, 4) * PAIR, PAIR)
            return jnp.where(lax.div(chip, 4) == zh, near[:, pl.ds(at, PAIR)], far[:, pl.ds(at, PAIR)])

        left = [columns(d) for d in (0, 4, -1, 1, -2, 2, -3, 3)]
        j = lax.bitwise_xor(z, own_z)
        right = [own_ref[j], own_ref[NZL + j], r4[j], r4[NZL + j]]
        for step, ref in enumerate((r1, r2, r3)):
            at = 2 * NZL * step + j
            right += [ref[j], ref[NZL + j], swapped[at], swapped[at + NZL]]
        total += jnp.dot(
            jnp.concatenate(left, axis=1),
            jnp.concatenate(right, axis=0),
            preferred_element_type=F32,
        )
    o_ref[...] = (total * scale).astype(BF)


def project(near, far, ring, swapped, scale):
    rows = near[0].shape[0]
    cols = ring[0].shape[-1]
    full = pl.BlockSpec(memory_space=pltpu.VMEM)
    operands = [*near, *far, *ring, swapped]
    return pl.pallas_call(
        lambda *refs: project_body(*refs, scale=scale),
        out_shape=jax.ShapeDtypeStruct((rows, cols), BF),
        in_specs=[full] * len(operands),
        out_specs=full,
        cost_estimate=pl.CostEstimate(
            flops=2 * rows * 4096 * cols,
            bytes_accessed=2 * (rows * 4096 + cols * 4096 + rows * cols),
            transcendentals=0,
        ),
        compiler_params=pltpu.CompilerParams(vmem_limit_bytes=20 * MIB),
        name="project",
    )(*operands)


def ring_y(block):
    out = [block]
    for _ in range(4):
        out.append(hop(out[-1], dy=1, by_core=True))
    return out


def ring_x(block):
    one = hop(block, dx=1, by_core=True)
    three = hop(block, dx=3, by_core=True)
    two = hop(one, dx=1, by_core=True)
    return [block, one, two, three]


def join_body(*refs):
    *parts, o_ref = refs
    n = parts[0].shape[0]
    for i, part in enumerate(parts):
        o_ref[i * n : (i + 1) * n] = part[...]


def joined_blocks(blocks):
    full = pl.BlockSpec(memory_space=pltpu.VMEM)
    shape = (len(blocks) * blocks[0].shape[0],) + blocks[0].shape[1:]
    return pl.pallas_call(
        join_body,
        out_shape=jax.ShapeDtypeStruct(shape, BF),
        in_specs=[full] * len(blocks),
        out_specs=full,
        cost_estimate=pl.CostEstimate(flops=0, bytes_accessed=4 * 2**20, transcendentals=0),
        compiler_params=pltpu.CompilerParams(vmem_limit_bytes=8 * MIB),
        name="join",
    )(*blocks)


def gather_zcore(w):
    w = w[None]
    line = joined_blocks([w] + [hop(w, flip=j) for j in (1, 2, 3)])
    chips = [
        [z * 2 * NY + 2 * y + core for core in range(2)] for z in range(NZL) for y in range(NY)
    ]
    w = lax.all_gather(line, "ctx", axis=0, tiled=False, axis_index_groups=chips)
    return w.reshape((2 * NZL,) + w.shape[2:])


TILE = 256
REACH = 5 * TILE


def scores_body(len_ref, q_ref, own, e1, e2, g_ref, p_ref, dk0, dk1, dk2, ext, s_ref, d_ref, acc):
    rows = q_ref.shape[0]
    ext[0:rows] = e2[...]
    ext[rows : 2 * rows] = e1[...]
    ext[2 * rows : 3 * rows] = own[...]
    acc[...] = jnp.zeros_like(acc)
    docs = len_ref.shape[1]
    lead = lax.axis_index("ctx").astype(jnp.int32) * rows
    i0 = lax.broadcasted_iota(jnp.int32, (docs, docs), 0)
    i1 = lax.broadcasted_iota(jnp.int32, (docs, docs), 1)
    starts = jnp.sum(jnp.where(i1 < i0, len_ref[...], 0), axis=1, keepdims=True)

    @pl.loop(0, 4)
    def _(step):
        i, h = lax.rem(step, 2), lax.div(step, 2)
        row0 = pl.multiple_of(i * TILE, TILE)
        col0 = pl.multiple_of(h * HEAD_SIZE, HEAD_SIZE)
        q = q_ref[pl.ds(row0, TILE), pl.ds(col0, HEAD_SIZE)]
        g = g_ref[pl.ds(row0, TILE), pl.ds(col0, HEAD_SIZE)]
        row = row0 + lax.broadcasted_iota(jnp.int32, (1, TILE), 1)
        at = lead + row
        begin = jnp.max(jnp.where(starts <= at, starts, 0), axis=0, keepdims=True)
        low = jnp.maximum(begin - lead + WINDOW, row + 1)
        nt = (((1,), (1,)), ((), ()))
        peak = jnp.full((1, TILE), -1e30, F32)
        for j in range(5):
            first = pl.multiple_of(row0 + j * TILE, TILE)
            s = lax.dot_general(ext[pl.ds(first, TILE), :HEAD_SIZE], q, nt, preferred_element_type=F32)
            key = first + lax.broadcasted_iota(jnp.int32, (TILE, 1), 0)
            ok = key >= low
            if j == 4:
                ok = ok & (key <= row + WINDOW)
            s = jnp.where(ok, s, -1e30)
            s_ref[j * TILE : (j + 1) * TILE] = s
            peak = jnp.maximum(peak, jnp.max(s, axis=0, keepdims=True))
        total = jnp.zeros((1, TILE), F32)
        for j in range(5):
            e = jnp.exp(s_ref[j * TILE : (j + 1) * TILE] - peak)
            s_ref[j * TILE : (j + 1) * TILE] = e
            total += jnp.sum(e, axis=0, keepdims=True)
        inverse = 1.0 / total
        delta = jnp.zeros((1, TILE), F32)
        for j in range(5):
            first = pl.multiple_of(row0 + j * TILE, TILE)
            d = lax.dot_general(ext[pl.ds(first, TILE), HEAD_SIZE:], g, nt, preferred_element_type=F32)
            p = s_ref[j * TILE : (j + 1) * TILE] * inverse
            s_ref[j * TILE : (j + 1) * TILE] = p
            d_ref[j * TILE : (j + 1) * TILE] = d
            p_ref[step, j * TILE : (j + 1) * TILE] = p.astype(BF)
            delta += jnp.sum(p * d, axis=0, keepdims=True)
        for j in range(5):
            first = pl.multiple_of(row0 + j * TILE, TILE)
            part = slice(j * TILE, (j + 1) * TILE)
            ds = (s_ref[part] * (d_ref[part] - delta)).astype(BF)
            acc[pl.ds(first, TILE)] += jnp.dot(ds, q, preferred_element_type=F32)

    dk2[...] = acc[0:rows].astype(BF)
    dk1[...] = acc[rows : 2 * rows].astype(BF)
    dk0[...] = acc[2 * rows : 3 * rows]


def values_body(p_ref, own, e1, e2, o_ref):
    tn = (((0,), (0,)), ((), ()))
    for i in range(2):
        value = jnp.concatenate(
            [e2[i * TILE :, HEAD_SIZE:], e1[:, HEAD_SIZE:], own[: (i + 1) * TILE, HEAD_SIZE:]], axis=0
        )
        for h in range(2):
            a = lax.dot_general(p_ref[2 * h + i], value, tn, preferred_element_type=F32)
            o_ref[i * TILE : (i + 1) * TILE, h * HEAD_SIZE : (h + 1) * HEAD_SIZE] = a.astype(BF)


def attend(lens, query, own, e1, e2, grad):
    rows = query.shape[0]
    full = pl.BlockSpec(memory_space=pltpu.VMEM)
    shape = jax.ShapeDtypeStruct
    pairs = 4 * TILE * REACH
    p, dk0, dk1, dk2 = pl.pallas_call(
        scores_body,
        out_shape=(
            shape((4, REACH, TILE), BF),
            shape((rows, HEAD_SIZE), F32),
            shape((rows, HEAD_SIZE), BF),
            shape((rows, HEAD_SIZE), BF),
        ),
        in_specs=[full] * 6,
        out_specs=(full,) * 4,
        scratch_shapes=[
            pltpu.VMEM((3 * rows, 2 * HEAD_SIZE), BF),
            pltpu.VMEM((REACH, TILE), F32),
            pltpu.VMEM((REACH, TILE), F32),
            pltpu.VMEM((3 * rows, HEAD_SIZE), F32),
        ],
        cost_estimate=pl.CostEstimate(
            flops=6 * pairs * HEAD_SIZE, bytes_accessed=5 * rows * 1024 + 2 * pairs, transcendentals=pairs
        ),
        compiler_params=pltpu.CompilerParams(vmem_limit_bytes=16 * MIB),
        name="scores",
    )(lens, query, own, e1, e2, grad)
    out = pl.pallas_call(
        values_body,
        out_shape=shape((rows, 2 * HEAD_SIZE), BF),
        in_specs=[full] * 4,
        out_specs=full,
        cost_estimate=pl.CostEstimate(
            flops=2 * pairs * HEAD_SIZE, bytes_accessed=4 * rows * 1024 + 2 * pairs, transcendentals=0
        ),
        compiler_params=pltpu.CompilerParams(vmem_limit_bytes=14 * MIB),
        name="values",
    )(p, own, e1, e2)
    return out, dk0, dk1, dk2


def local(tokens, w_query, key_matrix, value_matrix, d_attended, doc_lengths):
    feature = jnp.arange(tokens.shape[1], dtype=jnp.int32)
    target = feature // ROWS * PAD + feature % ROWS
    spread = (target[:, None] == jnp.arange(8 * PAD, dtype=jnp.int32)[None, :]).astype(BF)
    own = jnp.dot(tokens, spread, preferred_element_type=F32).astype(BF)

    partner = hop(own, dz=NZL)
    near = ring_x(own)
    far = ring_x(partner)

    w = gather_zcore(jnp.concatenate([key_matrix, value_matrix, w_query], axis=1))
    w = jnp.pad(w, ((0, 0), (0, PAD - ROWS), (0, 0)))
    kv_cols = 2 * HEAD_SIZE
    kv = ring_y(w[..., :kv_cols])
    kv_a = hop(joined_blocks(kv[1:4]), swap=1)
    qs = ring_y(w[..., kv_cols:])
    q_a = hop(joined_blocks(qs[1:4]), swap=1)

    joined = project(near, far, kv, kv_a, 1.0)
    query = project(near, far, qs, q_a, 0.0625)

    e2 = along_ctx(joined, 2)
    e1 = along_ctx(joined, 1)
    attended, dk0, dk1, dk2 = attend(
        doc_lengths.reshape(1, -1), query, joined, e1, e2, d_attended
    )
    key_total = dk0 + along_ctx(dk2, -2).astype(F32) + along_ctx(dk1, -1).astype(F32)
    return (attended, key_total.astype(BF))


def solution(mesh):
    return jax.shard_map(
        local,
        mesh=mesh,
        in_specs=(
            P("ctx", "head"),
            P("ctx", "head"),
            P("ctx", "head"),
            P("ctx", "head"),
            P("ctx", "head"),
            P(),
        ),
        out_specs=(P("ctx", "head"), P("ctx", "head")),
        check_vma=False,
    )
```

```python
import jax
import jax.numpy as jnp
from jax import lax
from jax.experimental import pallas as pl
from jax.experimental.pallas import tpu as pltpu
from jax.sharding import PartitionSpec as P


HEAD_SIZE = 256
WINDOW = 1024
NX, NY, NZL, NZH = 4, 8, 4, 2
NZ = NZL * NZH
ROWS = 60
PAD = 64
PAIR = 2 * PAD
BOTH = ("ctx", "head")
BF = jnp.bfloat16
F32 = jnp.float32
MIB = 1024 * 1024


def place(x, y, z, core):
    x, y, z = x % NX, y % NY, z % NZ
    ctx = (z % NZL) * 2 * NY + 2 * y + core
    return ctx * (NX * NZH) + x * NZH + z // NZL


def hop(block, dx=0, dy=0, dz=0, swap=0, by_core=False, flip=0):
    route = []
    for x in range(NX):
        for y in range(NY):
            for z in range(NZ):
                for core in range(2):
                    s = 1 - 2 * core if by_core else 1
                    route.append(
                        (
                            place(x, y, z, core),
                            place(x + s * dx, y + s * dy, (z ^ flip) + s * dz, core ^ swap),
                        )
                    )
    return lax.ppermute(block, BOTH, route)


def along_ctx(block, distance):
    n = lax.axis_size("ctx")
    route = [(i - distance, i) for i in range(n) if 0 <= i - distance < n]
    return lax.ppermute(block, "ctx", route)


def project_body(t0, t1, t2, t3, p0, p1, p2, p3, own_ref, r1, r2, r3, r4, swapped, o_ref, *, scale):
    ctx = lax.axis_index("ctx").astype(jnp.int32)
    head = lax.axis_index("head").astype(jnp.int32)
    y = lax.rem(lax.div(ctx, 2), NY)
    own_z = lax.div(ctx, 2 * NY)
    sign = 1 - 2 * lax.rem(ctx, 2)
    x, zh = lax.div(head, NZH), lax.rem(head, NZH)
    total = jnp.zeros(o_ref.shape, F32)

    for slot, (near, far) in enumerate(((t0, p0), (t1, p1), (t2, p2), (t3, p3))):
        z = lax.rem(x - sign * slot + NX, NX)

        def columns(distance):
            chip = lax.rem(y + sign * distance + NY, NY)
            at = pl.multiple_of(lax.rem(chip, 4) * PAIR, PAIR)
            return jnp.where(lax.div(chip, 4) == zh, near[:, pl.ds(at, PAIR)], far[:, pl.ds(at, PAIR)])

        left = [columns(d) for d in (0, 4, -1, 1, -2, 2, -3, 3)]
        j = lax.bitwise_xor(z, own_z)
        right = [own_ref[j], own_ref[NZL + j], r4[j], r4[NZL + j]]
        for step, ref in enumerate((r1, r2, r3)):
            at = 2 * NZL * step + j
            right += [ref[j], ref[NZL + j], swapped[at], swapped[at + NZL]]
        total += jnp.dot(
            jnp.concatenate(left, axis=1),
            jnp.concatenate(right, axis=0),
            preferred_element_type=F32,
        )
    o_ref[...] = (total * scale).astype(BF)


def project(near, far, ring, swapped, scale):
    rows = near[0].shape[0]
    cols = ring[0].shape[-1]
    full = pl.BlockSpec(memory_space=pltpu.VMEM)
    operands = [*near, *far, *ring, swapped]
    return pl.pallas_call(
        lambda *refs: project_body(*refs, scale=scale),
        out_shape=jax.ShapeDtypeStruct((rows, cols), BF),
        in_specs=[full] * len(operands),
        out_specs=full,
        cost_estimate=pl.CostEstimate(
            flops=2 * rows * 4096 * cols,
            bytes_accessed=2 * (rows * 4096 + cols * 4096 + rows * cols),
            transcendentals=0,
        ),
        compiler_params=pltpu.CompilerParams(vmem_limit_bytes=20 * MIB),
        name="project",
    )(*operands)


def ring_y(block):
    out = [block]
    for _ in range(4):
        out.append(hop(out[-1], dy=1, by_core=True))
    return out


def ring_x(block):
    one = hop(block, dx=1, by_core=True)
    three = hop(block, dx=3, by_core=True)
    two = hop(one, dx=1, by_core=True)
    return [block, one, two, three]


def join_body(*refs):
    *parts, o_ref = refs
    n = parts[0].shape[0]
    for i, part in enumerate(parts):
        o_ref[i * n : (i + 1) * n] = part[...]


def joined_blocks(blocks):
    full = pl.BlockSpec(memory_space=pltpu.VMEM)
    shape = (len(blocks) * blocks[0].shape[0],) + blocks[0].shape[1:]
    return pl.pallas_call(
        join_body,
        out_shape=jax.ShapeDtypeStruct(shape, BF),
        in_specs=[full] * len(blocks),
        out_specs=full,
        cost_estimate=pl.CostEstimate(flops=0, bytes_accessed=4 * 2**20, transcendentals=0),
        compiler_params=pltpu.CompilerParams(vmem_limit_bytes=8 * MIB),
        name="join",
    )(*blocks)


def gather_zcore(w):
    w = w[None]
    line = joined_blocks([w] + [hop(w, flip=j) for j in (1, 2, 3)])
    chips = [
        [z * 2 * NY + 2 * y + core for core in range(2)] for z in range(NZL) for y in range(NY)
    ]
    w = lax.all_gather(line, "ctx", axis=0, tiled=False, axis_index_groups=chips)
    return w.reshape((2 * NZL,) + w.shape[2:])


TILE = 256
REACH = 5 * TILE


NT = (((1,), (1,)), ((), ()))


def tile_at(i, h):
    col0 = pl.multiple_of(h * HEAD_SIZE, HEAD_SIZE)
    return slice(i * TILE, (i + 1) * TILE), pl.ds(col0, HEAD_SIZE)


def first_allowed(len_ref, rows, row):
    docs = len_ref.shape[1]
    lead = lax.axis_index("ctx").astype(jnp.int32) * rows
    i0 = lax.broadcasted_iota(jnp.int32, (docs, docs), 0)
    i1 = lax.broadcasted_iota(jnp.int32, (docs, docs), 1)
    starts = jnp.sum(jnp.where(i1 < i0, len_ref[...], 0), axis=1, keepdims=True)
    begin = jnp.max(jnp.where(starts <= lead + row, starts, 0), axis=0, keepdims=True)
    return jnp.maximum(begin - lead + WINDOW, row + 1)


def block_scores(keys, q, first, low, high):
    s = lax.dot_general(keys, q, NT, preferred_element_type=F32)
    key = first + lax.broadcasted_iota(jnp.int32, (TILE, 1), 0)
    return jnp.where((key >= low) & (key <= high), s, -1e30)


def span(k):
    return slice(k * TILE, (k + 1) * TILE)


def near_body(len_ref, q_ref, own, e1, g_ref, e_ref, d_ref, stat_ref):
    rows = q_ref.shape[0]
    for i in range(2):

        @pl.loop(0, 2)
        def _(h):
            step = 2 * h + i
            q, g = q_ref[tile_at(i, h)], g_ref[tile_at(i, h)]
            row = i * TILE + lax.broadcasted_iota(jnp.int32, (1, TILE), 1)
            low = first_allowed(len_ref, rows, row) - rows
            high = row + (WINDOW - rows)
            peak = jnp.full((1, TILE), -1e30, F32)
            for k in range(3 + i):
                keys = (e1 if k < 2 else own)[span(k % 2), :HEAD_SIZE]
                s = block_scores(keys, q, k * TILE, low, high)
                e_ref[step, span(k)] = s
                peak = jnp.maximum(peak, jnp.max(s, axis=0, keepdims=True))
            total = jnp.zeros((1, TILE), F32)
            weighted = jnp.zeros((1, TILE), F32)
            for k in range(3 + i):
                values = (e1 if k < 2 else own)[span(k % 2), HEAD_SIZE:]
                d = lax.dot_general(values, g, NT, preferred_element_type=F32)
                e = jnp.exp(e_ref[step, span(k)] - peak)
                e_ref[step, span(k)] = e
                d_ref[step, span(k)] = d
                total += jnp.sum(e, axis=0, keepdims=True)
                weighted += jnp.sum(e * d, axis=0, keepdims=True)
            stat_ref[step, 0:1] = peak
            stat_ref[step, 1:2] = total
            stat_ref[step, 2:3] = weighted


def far_body(len_ref, q_ref, e2, g_ref, e_ref, d_ref, stat_ref, p_ref, dk0, dk1, dk2, s_ref, t_ref, acc):
    rows = q_ref.shape[0]
    acc[...] = jnp.zeros_like(acc)
    for i in range(2):

        @pl.loop(0, 2)
        def _(h):
            step = 2 * h + i
            q, g = q_ref[tile_at(i, h)], g_ref[tile_at(i, h)]
            row = i * TILE + lax.broadcasted_iota(jnp.int32, (1, TILE), 1)
            low = first_allowed(len_ref, rows, row)
            near_peak = stat_ref[step, 0:1]
            peak = near_peak
            for k in range(i, 2):
                s = block_scores(e2[span(k), :HEAD_SIZE], q, k * TILE, low, 2 * rows)
                s_ref[span(k)] = s
                peak = jnp.maximum(peak, jnp.max(s, axis=0, keepdims=True))
            shrink = jnp.exp(near_peak - peak)
            total = stat_ref[step, 1:2] * shrink
            weighted = stat_ref[step, 2:3] * shrink
            for k in range(i, 2):
                d = lax.dot_general(e2[span(k), HEAD_SIZE:], g, NT, preferred_element_type=F32)
                e = jnp.exp(s_ref[span(k)] - peak)
                s_ref[span(k)] = e
                t_ref[span(k)] = d
                total += jnp.sum(e, axis=0, keepdims=True)
                weighted += jnp.sum(e * d, axis=0, keepdims=True)
            inverse = 1.0 / total
            delta = weighted * inverse
            near_scale = shrink * inverse
            for k in range(i, i + 5):
                if k < 2:
                    p, d = s_ref[span(k)] * inverse, t_ref[span(k)]
                else:
                    p, d = e_ref[step, span(k - 2)] * near_scale, d_ref[step, span(k - 2)]
                p_ref[step, span(k - i)] = p.astype(BF)
                ds = (p * (d - delta)).astype(BF)
                acc[span(k)] += jnp.dot(ds, q, preferred_element_type=F32)

    dk2[...] = acc[0:rows].astype(BF)
    dk1[...] = acc[rows : 2 * rows].astype(BF)
    dk0[...] = acc[2 * rows : 3 * rows]


def values_body(p_ref, own, e1, e2, o_ref):
    tn = (((0,), (0,)), ((), ()))
    for i in range(2):
        value = jnp.concatenate(
            [e2[i * TILE :, HEAD_SIZE:], e1[:, HEAD_SIZE:], own[: (i + 1) * TILE, HEAD_SIZE:]], axis=0
        )
        for h in range(2):
            a = lax.dot_general(p_ref[2 * h + i], value, tn, preferred_element_type=F32)
            o_ref[i * TILE : (i + 1) * TILE, h * HEAD_SIZE : (h + 1) * HEAD_SIZE] = a.astype(BF)


def attend(lens, query, own, e1, e2, grad):
    rows = query.shape[0]
    full = pl.BlockSpec(memory_space=pltpu.VMEM)
    shape = jax.ShapeDtypeStruct
    pairs = 4 * TILE * REACH
    e, d, stat = pl.pallas_call(
        near_body,
        out_shape=(
            shape((4, 2 * rows, TILE), F32),
            shape((4, 2 * rows, TILE), F32),
            shape((4, 8, TILE), F32),
        ),
        in_specs=[full] * 5,
        out_specs=(full,) * 3,
        cost_estimate=pl.CostEstimate(
            flops=3 * pairs * HEAD_SIZE, bytes_accessed=5 * rows * 1024 + 8 * pairs, transcendentals=pairs
        ),
        compiler_params=pltpu.CompilerParams(vmem_limit_bytes=16 * MIB),
        name="near_scores",
    )(lens, query, own, e1, grad)
    p, dk0, dk1, dk2 = pl.pallas_call(
        far_body,
        out_shape=(
            shape((4, REACH, TILE), BF),
            shape((rows, HEAD_SIZE), F32),
            shape((rows, HEAD_SIZE), BF),
            shape((rows, HEAD_SIZE), BF),
        ),
        in_specs=[full] * 7,
        out_specs=(full,) * 4,
        scratch_shapes=[
            pltpu.VMEM((rows, TILE), F32),
            pltpu.VMEM((rows, TILE), F32),
            pltpu.VMEM((3 * rows, HEAD_SIZE), F32),
        ],
        cost_estimate=pl.CostEstimate(
            flops=3 * pairs * HEAD_SIZE, bytes_accessed=5 * rows * 1024 + 10 * pairs, transcendentals=pairs
        ),
        compiler_params=pltpu.CompilerParams(vmem_limit_bytes=20 * MIB),
        name="far_scores",
    )(lens, query, e2, grad, e, d, stat)
    out = pl.pallas_call(
        values_body,
        out_shape=shape((rows, 2 * HEAD_SIZE), BF),
        in_specs=[full] * 4,
        out_specs=full,
        cost_estimate=pl.CostEstimate(
            flops=2 * pairs * HEAD_SIZE, bytes_accessed=4 * rows * 1024 + 2 * pairs, transcendentals=0
        ),
        compiler_params=pltpu.CompilerParams(vmem_limit_bytes=14 * MIB),
        name="values",
    )(p, own, e1, e2)
    return out, dk0, dk1, dk2


def local(tokens, w_query, key_matrix, value_matrix, d_attended, doc_lengths):
    feature = jnp.arange(tokens.shape[1], dtype=jnp.int32)
    target = feature // ROWS * PAD + feature % ROWS
    spread = (target[:, None] == jnp.arange(8 * PAD, dtype=jnp.int32)[None, :]).astype(BF)
    own = jnp.dot(tokens, spread, preferred_element_type=F32).astype(BF)

    partner = hop(own, dz=NZL)
    near = ring_x(own)
    far = ring_x(partner)

    w = gather_zcore(jnp.concatenate([key_matrix, value_matrix, w_query], axis=1))
    w = jnp.pad(w, ((0, 0), (0, PAD - ROWS), (0, 0)))
    kv_cols = 2 * HEAD_SIZE
    kv = ring_y(w[..., :kv_cols])
    kv_a = hop(joined_blocks(kv[1:4]), swap=1)
    qs = ring_y(w[..., kv_cols:])
    q_a = hop(joined_blocks(qs[1:4]), swap=1)

    joined = project(near, far, kv, kv_a, 1.0)
    query = project(near, far, qs, q_a, 0.0625)

    e2 = along_ctx(joined, 2)
    e1 = along_ctx(joined, 1)
    attended, dk0, dk1, dk2 = attend(
        doc_lengths.reshape(1, -1), query, joined, e1, e2, d_attended
    )
    key_total = dk0 + along_ctx(dk2, -2).astype(F32) + along_ctx(dk1, -1).astype(F32)
    return (attended, key_total.astype(BF))


def solution(mesh):
    return jax.shard_map(
        local,
        mesh=mesh,
        in_specs=(
            P("ctx", "head"),
            P("ctx", "head"),
            P("ctx", "head"),
            P("ctx", "head"),
            P("ctx", "head"),
            P(),
        ),
        out_specs=(P("ctx", "head"), P("ctx", "head")),
        check_vma=False,
    )
```

```python
import jax
import jax.numpy as jnp
from jax import lax
from jax.experimental import pallas as pl
from jax.experimental.pallas import tpu as pltpu
from jax.sharding import PartitionSpec as P


HEAD_SIZE = 256
WINDOW = 1024
NX, NY, NZL, NZH = 4, 8, 4, 2
NZ = NZL * NZH
ROWS = 60
PAD = 64
PAIR = 2 * PAD
BOTH = ("ctx", "head")
BF = jnp.bfloat16
F32 = jnp.float32
MIB = 1024 * 1024


def place(x, y, z, core):
    x, y, z = x % NX, y % NY, z % NZ
    ctx = (z % NZL) * 2 * NY + 2 * y + core
    return ctx * (NX * NZH) + x * NZH + z // NZL


def hop(block, dx=0, dy=0, dz=0, swap=0, by_core=False, flip=0):
    route = []
    for x in range(NX):
        for y in range(NY):
            for z in range(NZ):
                for core in range(2):
                    s = 1 - 2 * core if by_core else 1
                    route.append(
                        (
                            place(x, y, z, core),
                            place(x + s * dx, y + s * dy, (z ^ flip) + s * dz, core ^ swap),
                        )
                    )
    return lax.ppermute(block, BOTH, route)


def along_ctx(block, distance):
    n = lax.axis_size("ctx")
    route = [(i - distance, i) for i in range(n) if 0 <= i - distance < n]
    return lax.ppermute(block, "ctx", route)


def project_body(*refs, slots, scale):
    count = len(slots)
    near, far = refs[:count], refs[count : 2 * count]
    own_ref, r1, r2, r3, r4, swapped = refs[2 * count : 2 * count + 6]
    *sums, o_ref = refs[2 * count + 6 :]
    ctx = lax.axis_index("ctx").astype(jnp.int32)
    head = lax.axis_index("head").astype(jnp.int32)
    y = lax.rem(lax.div(ctx, 2), NY)
    sign = 1 - 2 * lax.rem(ctx, 2)
    x, zh = lax.div(head, NZH), lax.rem(head, NZH)
    total = sums[0][...] if sums else jnp.zeros(o_ref.shape, F32)

    for slot, near_ref, far_ref in zip(slots, near, far):
        z = lax.rem(x - sign * slot + NX, NX)

        def columns(distance):
            chip = lax.rem(y + sign * distance + NY, NY)
            at = pl.multiple_of(lax.rem(chip, 4) * PAIR, PAIR)
            mine = near_ref[:, pl.ds(at, PAIR)]
            return jnp.where(lax.div(chip, 4) == zh, mine, far_ref[:, pl.ds(at, PAIR)])

        left = [columns(d) for d in (0, 4, -1, 1, -2, 2, -3, 3)]
        right = [own_ref[z], own_ref[NZL + z], r4[z], r4[NZL + z]]
        for step, ref in enumerate((r1, r2, r3)):
            at = 2 * NZL * step + z
            right += [ref[z], ref[NZL + z], swapped[at], swapped[at + NZL]]
        total += jnp.dot(
            jnp.concatenate(left, axis=1),
            jnp.concatenate(right, axis=0),
            preferred_element_type=F32,
        )
    o_ref[...] = (total * scale).astype(o_ref.dtype)


def project(near, far, ring, swapped, scale, slots=(0, 1, 2, 3), sums=(), dtype=BF):
    rows = near[0].shape[0]
    cols = ring[0].shape[-1]
    full = pl.BlockSpec(memory_space=pltpu.VMEM)
    operands = [near[i] for i in slots] + [far[i] for i in slots] + [*ring, swapped, *sums]
    depth = 1024 * len(slots)
    return pl.pallas_call(
        lambda *refs: project_body(*refs, slots=slots, scale=scale),
        out_shape=jax.ShapeDtypeStruct((rows, cols), dtype),
        in_specs=[full] * len(operands),
        out_specs=full,
        cost_estimate=pl.CostEstimate(
            flops=2 * rows * depth * cols,
            bytes_accessed=2 * (rows * depth + cols * depth + rows * cols),
            transcendentals=0,
        ),
        compiler_params=pltpu.CompilerParams(vmem_limit_bytes=20 * MIB),
        name="project",
    )(*operands)


def ring_y(block):
    out = [block]
    for _ in range(4):
        out.append(hop(out[-1], dy=1, by_core=True))
    return out


def ring_x(block):
    one = hop(block, dx=1, by_core=True)
    three = hop(block, dx=3, by_core=True)
    two = hop(one, dx=1, by_core=True)
    return [block, one, two, three]


def join_body(*refs):
    *parts, o_ref = refs
    n = parts[0].shape[0]
    for i, part in enumerate(parts):
        o_ref[i * n : (i + 1) * n] = part[...]


def joined_blocks(blocks):
    full = pl.BlockSpec(memory_space=pltpu.VMEM)
    shape = (len(blocks) * blocks[0].shape[0],) + blocks[0].shape[1:]
    return pl.pallas_call(
        join_body,
        out_shape=jax.ShapeDtypeStruct(shape, BF),
        in_specs=[full] * len(blocks),
        out_specs=full,
        cost_estimate=pl.CostEstimate(flops=0, bytes_accessed=4 * 2**20, transcendentals=0),
        compiler_params=pltpu.CompilerParams(vmem_limit_bytes=8 * MIB),
        name="join",
    )(*blocks)


def gather_zcore(w):
    def index(z, y, core):
        return z * 2 * NY + 2 * y + core

    lines = [[index(z, y, core) for z in range(NZL)] for y in range(NY) for core in range(2)]
    chips = [[index(z, y, core) for core in range(2)] for z in range(NZL) for y in range(NY)]
    w = lax.all_gather(w, "ctx", axis=0, tiled=False, axis_index_groups=lines)
    w = lax.all_gather(w, "ctx", axis=0, tiled=False, axis_index_groups=chips)
    return w.reshape((2 * NZL,) + w.shape[2:])


TILE = 256
REACH = 5 * TILE


NT = (((1,), (1,)), ((), ()))


def tile_at(i, h):
    col0 = pl.multiple_of(h * HEAD_SIZE, HEAD_SIZE)
    return slice(i * TILE, (i + 1) * TILE), pl.ds(col0, HEAD_SIZE)


def first_allowed(len_ref, rows, row):
    docs = len_ref.shape[1]
    lead = lax.axis_index("ctx").astype(jnp.int32) * rows
    i0 = lax.broadcasted_iota(jnp.int32, (docs, docs), 0)
    i1 = lax.broadcasted_iota(jnp.int32, (docs, docs), 1)
    starts = jnp.sum(jnp.where(i1 < i0, len_ref[...], 0), axis=1, keepdims=True)
    begin = jnp.max(jnp.where(starts <= lead + row, starts, 0), axis=0, keepdims=True)
    return jnp.maximum(begin - lead + WINDOW, row + 1)


def block_scores(keys, q, first, low, high):
    s = lax.dot_general(keys, q, NT, preferred_element_type=F32)
    key = first + lax.broadcasted_iota(jnp.int32, (TILE, 1), 0)
    return jnp.where((key >= low) & (key <= high), s, -1e30)


def span(k):
    return slice(k * TILE, (k + 1) * TILE)


def near_body(len_ref, q_ref, own, e1, g_ref, e_ref, d_ref, stat_ref):
    rows = q_ref.shape[0]
    for i in range(2):

        @pl.loop(0, 2)
        def _(h):
            step = 2 * h + i
            q, g = q_ref[tile_at(i, h)], g_ref[tile_at(i, h)]
            row = i * TILE + lax.broadcasted_iota(jnp.int32, (1, TILE), 1)
            low = first_allowed(len_ref, rows, row) - rows
            high = row + (WINDOW - rows)
            peak = jnp.full((1, TILE), -1e30, F32)
            for k in range(3 + i):
                keys = (e1 if k < 2 else own)[span(k % 2), :HEAD_SIZE]
                s = block_scores(keys, q, k * TILE, low, high)
                e_ref[step, span(k)] = s
                peak = jnp.maximum(peak, jnp.max(s, axis=0, keepdims=True))
            total = jnp.zeros((1, TILE), F32)
            weighted = jnp.zeros((1, TILE), F32)
            for k in range(3 + i):
                values = (e1 if k < 2 else own)[span(k % 2), HEAD_SIZE:]
                d = lax.dot_general(values, g, NT, preferred_element_type=F32)
                e = jnp.exp(e_ref[step, span(k)] - peak)
                e_ref[step, span(k)] = e
                d_ref[step, span(k)] = d
                total += jnp.sum(e, axis=0, keepdims=True)
                weighted += jnp.sum(e * d, axis=0, keepdims=True)
            stat_ref[step, 0:1] = peak
            stat_ref[step, 1:2] = total
            stat_ref[step, 2:3] = weighted


def far_body(len_ref, q_ref, e2, g_ref, e_ref, d_ref, stat_ref, p_ref, dk0, dk1, dk2, s_ref, t_ref, acc):
    rows = q_ref.shape[0]
    acc[...] = jnp.zeros_like(acc)
    for i in range(2):

        @pl.loop(0, 2)
        def _(h):
            step = 2 * h + i
            q, g = q_ref[tile_at(i, h)], g_ref[tile_at(i, h)]
            row = i * TILE + lax.broadcasted_iota(jnp.int32, (1, TILE), 1)
            low = first_allowed(len_ref, rows, row)
            near_peak = stat_ref[step, 0:1]
            peak = near_peak
            for k in range(i, 2):
                s = block_scores(e2[span(k), :HEAD_SIZE], q, k * TILE, low, 2 * rows)
                s_ref[span(k)] = s
                peak = jnp.maximum(peak, jnp.max(s, axis=0, keepdims=True))
            shrink = jnp.exp(near_peak - peak)
            total = stat_ref[step, 1:2] * shrink
            weighted = stat_ref[step, 2:3] * shrink
            for k in range(i, 2):
                d = lax.dot_general(e2[span(k), HEAD_SIZE:], g, NT, preferred_element_type=F32)
                e = jnp.exp(s_ref[span(k)] - peak)
                s_ref[span(k)] = e
                t_ref[span(k)] = d
                total += jnp.sum(e, axis=0, keepdims=True)
                weighted += jnp.sum(e * d, axis=0, keepdims=True)
            inverse = 1.0 / total
            delta = weighted * inverse
            near_scale = shrink * inverse
            for k in range(i, i + 5):
                if k < 2:
                    p, d = s_ref[span(k)] * inverse, t_ref[span(k)]
                else:
                    p, d = e_ref[step, span(k - 2)] * near_scale, d_ref[step, span(k - 2)]
                p_ref[step, span(k - i)] = p.astype(BF)
                ds = (p * (d - delta)).astype(BF)
                acc[span(k)] += jnp.dot(ds, q, preferred_element_type=F32)

    dk2[...] = acc[0:rows].astype(BF)
    dk1[...] = acc[rows : 2 * rows].astype(BF)
    dk0[...] = acc[2 * rows : 3 * rows]


def values_body(p_ref, own, e1, e2, o_ref):
    tn = (((0,), (0,)), ((), ()))
    for i in range(2):
        value = jnp.concatenate(
            [e2[i * TILE :, HEAD_SIZE:], e1[:, HEAD_SIZE:], own[: (i + 1) * TILE, HEAD_SIZE:]], axis=0
        )
        for h in range(2):
            a = lax.dot_general(p_ref[2 * h + i], value, tn, preferred_element_type=F32)
            o_ref[i * TILE : (i + 1) * TILE, h * HEAD_SIZE : (h + 1) * HEAD_SIZE] = a.astype(BF)


def attend(lens, query, own, e1, e2, grad):
    rows = query.shape[0]
    full = pl.BlockSpec(memory_space=pltpu.VMEM)
    shape = jax.ShapeDtypeStruct
    pairs = 4 * TILE * REACH
    e, d, stat = pl.pallas_call(
        near_body,
        out_shape=(
            shape((4, 2 * rows, TILE), F32),
            shape((4, 2 * rows, TILE), F32),
            shape((4, 8, TILE), F32),
        ),
        in_specs=[full] * 5,
        out_specs=(full,) * 3,
        cost_estimate=pl.CostEstimate(
            flops=3 * pairs * HEAD_SIZE, bytes_accessed=5 * rows * 1024 + 8 * pairs, transcendentals=pairs
        ),
        compiler_params=pltpu.CompilerParams(vmem_limit_bytes=16 * MIB),
        name="near_scores",
    )(lens, query, own, e1, grad)
    p, dk0, dk1, dk2 = pl.pallas_call(
        far_body,
        out_shape=(
            shape((4, REACH, TILE), BF),
            shape((rows, HEAD_SIZE), F32),
            shape((rows, HEAD_SIZE), BF),
            shape((rows, HEAD_SIZE), BF),
        ),
        in_specs=[full] * 7,
        out_specs=(full,) * 4,
        scratch_shapes=[
            pltpu.VMEM((rows, TILE), F32),
            pltpu.VMEM((rows, TILE), F32),
            pltpu.VMEM((3 * rows, HEAD_SIZE), F32),
        ],
        cost_estimate=pl.CostEstimate(
            flops=3 * pairs * HEAD_SIZE, bytes_accessed=5 * rows * 1024 + 10 * pairs, transcendentals=pairs
        ),
        compiler_params=pltpu.CompilerParams(vmem_limit_bytes=20 * MIB),
        name="far_scores",
    )(lens, query, e2, grad, e, d, stat)
    out = pl.pallas_call(
        values_body,
        out_shape=shape((rows, 2 * HEAD_SIZE), BF),
        in_specs=[full] * 4,
        out_specs=full,
        cost_estimate=pl.CostEstimate(
            flops=2 * pairs * HEAD_SIZE, bytes_accessed=4 * rows * 1024 + 2 * pairs, transcendentals=0
        ),
        compiler_params=pltpu.CompilerParams(vmem_limit_bytes=14 * MIB),
        name="values",
    )(p, own, e1, e2)
    return out, dk0, dk1, dk2


def local(tokens, w_query, key_matrix, value_matrix, d_attended, doc_lengths):
    feature = jnp.arange(tokens.shape[1], dtype=jnp.int32)
    target = feature // ROWS * PAD + feature % ROWS
    spread = (target[:, None] == jnp.arange(8 * PAD, dtype=jnp.int32)[None, :]).astype(BF)
    own = jnp.dot(tokens, spread, preferred_element_type=F32).astype(BF)

    partner = hop(own, dz=NZL)
    near = ring_x(own)
    far = ring_x(partner)

    w = gather_zcore(jnp.concatenate([key_matrix, value_matrix, w_query], axis=1))
    w = jnp.pad(w, ((0, 0), (0, PAD - ROWS), (0, 0)))
    kv_cols = 2 * HEAD_SIZE
    kv = ring_y(w[..., :kv_cols])
    kv_a = hop(joined_blocks(kv[1:4]), swap=1)
    qs = ring_y(w[..., kv_cols:])
    q_a = hop(joined_blocks(qs[1:4]), swap=1)

    sums = project(near, far, kv, kv_a, 1.0, slots=(0, 1, 3), dtype=F32)
    joined = project(near, far, kv, kv_a, 1.0, slots=(2,), sums=(sums,))
    query = project(near, far, qs, q_a, 0.0625)

    e2 = along_ctx(joined, 2)
    e1 = along_ctx(joined, 1)
    attended, dk0, dk1, dk2 = attend(
        doc_lengths.reshape(1, -1), query, joined, e1, e2, d_attended
    )
    key_total = dk0 + along_ctx(dk2, -2).astype(F32) + along_ctx(dk1, -1).astype(F32)
    return (attended, key_total.astype(BF))


def solution(mesh):
    return jax.shard_map(
        local,
        mesh=mesh,
        in_specs=(
            P("ctx", "head"),
            P("ctx", "head"),
            P("ctx", "head"),
            P("ctx", "head"),
            P("ctx", "head"),
            P(),
        ),
        out_specs=(P("ctx", "head"), P("ctx", "head")),
        check_vma=False,
    )
```

```python
import jax
import jax.numpy as jnp
from jax import lax
from jax.experimental import pallas as pl
from jax.experimental.pallas import tpu as pltpu
from jax.sharding import PartitionSpec as P


HEAD_SIZE = 256
WINDOW = 1024
NX, NY, NZL, NZH = 4, 8, 4, 2
NZ = NZL * NZH
ROWS = 60
PAD = 64
PAIR = 2 * PAD
BOTH = ("ctx", "head")
BF = jnp.bfloat16
F32 = jnp.float32
MIB = 1024 * 1024


def place(x, y, z, core):
    x, y, z = x % NX, y % NY, z % NZ
    ctx = (z % NZL) * 2 * NY + 2 * y + core
    return ctx * (NX * NZH) + x * NZH + z // NZL


def hop(block, dx=0, dy=0, dz=0, swap=0, by_core=False, flip=0):
    route = []
    for x in range(NX):
        for y in range(NY):
            for z in range(NZ):
                for core in range(2):
                    s = 1 - 2 * core if by_core else 1
                    route.append(
                        (
                            place(x, y, z, core),
                            place(x + s * dx, y + s * dy, (z ^ flip) + s * dz, core ^ swap),
                        )
                    )
    return lax.ppermute(block, BOTH, route)


def along_ctx(block, distance):
    n = lax.axis_size("ctx")
    route = [(i - distance, i) for i in range(n) if 0 <= i - distance < n]
    return lax.ppermute(block, "ctx", route)


def project_body(*refs, slots, scale):
    count = len(slots)
    near, far = refs[:count], refs[count : 2 * count]
    own_ref, r1, r2, r3, r4, swapped = refs[2 * count : 2 * count + 6]
    *sums, o_ref = refs[2 * count + 6 :]
    ctx = lax.axis_index("ctx").astype(jnp.int32)
    head = lax.axis_index("head").astype(jnp.int32)
    y = lax.rem(lax.div(ctx, 2), NY)
    sign = 1 - 2 * lax.rem(ctx, 2)
    x, zh = lax.div(head, NZH), lax.rem(head, NZH)
    total = sums[0][...] if sums else jnp.zeros(o_ref.shape, F32)

    for slot, near_ref, far_ref in zip(slots, near, far):
        z = lax.rem(x - sign * slot + NX, NX)

        def columns(distance):
            chip = lax.rem(y + sign * distance + NY, NY)
            at = pl.multiple_of(lax.rem(chip, 4) * PAIR, PAIR)
            mine = near_ref[:, pl.ds(at, PAIR)]
            return jnp.where(lax.div(chip, 4) == zh, mine, far_ref[:, pl.ds(at, PAIR)])

        left = [columns(d) for d in (0, 4, -1, 1, -2, 2, -3, 3)]
        right = [own_ref[z], own_ref[NZL + z], r4[z], r4[NZL + z]]
        for step, ref in enumerate((r1, r2, r3)):
            at = 2 * NZL * step + z
            right += [ref[z], ref[NZL + z], swapped[at], swapped[at + NZL]]
        total += jnp.dot(
            jnp.concatenate(left, axis=1),
            jnp.concatenate(right, axis=0),
            preferred_element_type=F32,
        )
    o_ref[...] = (total * scale).astype(o_ref.dtype)


def project(near, far, ring, swapped, scale, slots=(0, 1, 2, 3), sums=(), dtype=BF):
    rows = near[0].shape[0]
    cols = ring[0].shape[-1]
    full = pl.BlockSpec(memory_space=pltpu.VMEM)
    operands = [near[i] for i in slots] + [far[i] for i in slots] + [*ring, swapped, *sums]
    depth = 1024 * len(slots)
    return pl.pallas_call(
        lambda *refs: project_body(*refs, slots=slots, scale=scale),
        out_shape=jax.ShapeDtypeStruct((rows, cols), dtype),
        in_specs=[full] * len(operands),
        out_specs=full,
        cost_estimate=pl.CostEstimate(
            flops=2 * rows * depth * cols,
            bytes_accessed=2 * (rows * depth + cols * depth + rows * cols),
            transcendentals=0,
        ),
        compiler_params=pltpu.CompilerParams(vmem_limit_bytes=20 * MIB),
        name="project",
    )(*operands)


def split_body(w_ref, kv_ref, q_ref):
    cols = kv_ref.shape[-1]
    kv_ref[...] = w_ref[:, :, :cols]
    q_ref[...] = w_ref[:, :, cols:]


def split(w):
    full = pl.BlockSpec(memory_space=pltpu.VMEM)
    half = jax.ShapeDtypeStruct(w.shape[:2] + (2 * HEAD_SIZE,), BF)
    return pl.pallas_call(
        split_body,
        out_shape=(half, half),
        in_specs=[full],
        out_specs=(full, full),
        cost_estimate=pl.CostEstimate(flops=0, bytes_accessed=4 * 2**20, transcendentals=0),
        compiler_params=pltpu.CompilerParams(vmem_limit_bytes=8 * MIB),
        name="split",
    )(w)


def ring_y(block, first):
    out = [block, first]
    for _ in range(1, 4):
        out.append(hop(out[-1], dy=1, by_core=True))
    return out


def ring_x(block):
    one = hop(block, dx=1, by_core=True)
    three = hop(block, dx=3, by_core=True)
    two = hop(one, dx=1, by_core=True)
    return [block, one, two, three]


def join_body(*refs):
    *parts, o_ref = refs
    n = parts[0].shape[0]
    for i, part in enumerate(parts):
        o_ref[i * n : (i + 1) * n] = part[...]


def joined_blocks(blocks):
    full = pl.BlockSpec(memory_space=pltpu.VMEM)
    shape = (len(blocks) * blocks[0].shape[0],) + blocks[0].shape[1:]
    return pl.pallas_call(
        join_body,
        out_shape=jax.ShapeDtypeStruct(shape, BF),
        in_specs=[full] * len(blocks),
        out_specs=full,
        cost_estimate=pl.CostEstimate(flops=0, bytes_accessed=4 * 2**20, transcendentals=0),
        compiler_params=pltpu.CompilerParams(vmem_limit_bytes=8 * MIB),
        name="join",
    )(*blocks)


def gather_zcore(w):
    def index(z, y, core):
        return z * 2 * NY + 2 * y + core

    lines = [[index(z, y, core) for z in range(NZL)] for y in range(NY) for core in range(2)]
    chips = [[index(z, y, core) for core in range(2)] for z in range(NZL) for y in range(NY)]
    w = lax.all_gather(w, "ctx", axis=0, tiled=False, axis_index_groups=lines)
    w = lax.all_gather(w, "ctx", axis=0, tiled=False, axis_index_groups=chips)
    return w.reshape((2 * NZL,) + w.shape[2:])


TILE = 256
REACH = 5 * TILE


NT = (((1,), (1,)), ((), ()))


def tile_at(i, h):
    col0 = pl.multiple_of(h * HEAD_SIZE, HEAD_SIZE)
    return slice(i * TILE, (i + 1) * TILE), pl.ds(col0, HEAD_SIZE)


def first_allowed(len_ref, rows, row):
    docs = len_ref.shape[1]
    lead = lax.axis_index("ctx").astype(jnp.int32) * rows
    i0 = lax.broadcasted_iota(jnp.int32, (docs, docs), 0)
    i1 = lax.broadcasted_iota(jnp.int32, (docs, docs), 1)
    starts = jnp.sum(jnp.where(i1 < i0, len_ref[...], 0), axis=1, keepdims=True)
    begin = jnp.max(jnp.where(starts <= lead + row, starts, 0), axis=0, keepdims=True)
    return jnp.maximum(begin - lead + WINDOW, row + 1)


def block_scores(keys, q, first, low, high):
    s = lax.dot_general(keys, q, NT, preferred_element_type=F32)
    key = first + lax.broadcasted_iota(jnp.int32, (TILE, 1), 0)
    return jnp.where((key >= low) & (key <= high), s, -1e30)


def span(k):
    return slice(k * TILE, (k + 1) * TILE)


def near_body(len_ref, q_ref, own, e1, g_ref, e_ref, d_ref, stat_ref):
    rows = q_ref.shape[0]
    for i in range(2):

        @pl.loop(0, 2)
        def _(h):
            step = 2 * h + i
            q, g = q_ref[tile_at(i, h)], g_ref[tile_at(i, h)]
            row = i * TILE + lax.broadcasted_iota(jnp.int32, (1, TILE), 1)
            low = first_allowed(len_ref, rows, row) - rows
            high = row + (WINDOW - rows)
            peak = jnp.full((1, TILE), -1e30, F32)
            for k in range(3 + i):
                keys = (e1 if k < 2 else own)[span(k % 2), :HEAD_SIZE]
                s = block_scores(keys, q, k * TILE, low, high)
                e_ref[step, span(k)] = s
                peak = jnp.maximum(peak, jnp.max(s, axis=0, keepdims=True))
            total = jnp.zeros((1, TILE), F32)
            weighted = jnp.zeros((1, TILE), F32)
            for k in range(3 + i):
                values = (e1 if k < 2 else own)[span(k % 2), HEAD_SIZE:]
                d = lax.dot_general(values, g, NT, preferred_element_type=F32)
                e = jnp.exp(e_ref[step, span(k)] - peak)
                e_ref[step, span(k)] = e
                d_ref[step, span(k)] = d
                total += jnp.sum(e, axis=0, keepdims=True)
                weighted += jnp.sum(e * d, axis=0, keepdims=True)
            stat_ref[step, 0:1] = peak
            stat_ref[step, 1:2] = total
            stat_ref[step, 2:3] = weighted


def far_body(len_ref, q_ref, e2, g_ref, e_ref, d_ref, stat_ref, p_ref, dk0, dk1, dk2, s_ref, t_ref, acc):
    rows = q_ref.shape[0]
    acc[...] = jnp.zeros_like(acc)
    for i in range(2):

        @pl.loop(0, 2)
        def _(h):
            step = 2 * h + i
            q, g = q_ref[tile_at(i, h)], g_ref[tile_at(i, h)]
            row = i * TILE + lax.broadcasted_iota(jnp.int32, (1, TILE), 1)
            low = first_allowed(len_ref, rows, row)
            near_peak = stat_ref[step, 0:1]
            peak = near_peak
            for k in range(i, 2):
                s = block_scores(e2[span(k), :HEAD_SIZE], q, k * TILE, low, 2 * rows)
                s_ref[span(k)] = s
                peak = jnp.maximum(peak, jnp.max(s, axis=0, keepdims=True))
            shrink = jnp.exp(near_peak - peak)
            total = stat_ref[step, 1:2] * shrink
            weighted = stat_ref[step, 2:3] * shrink
            for k in range(i, 2):
                d = lax.dot_general(e2[span(k), HEAD_SIZE:], g, NT, preferred_element_type=F32)
                e = jnp.exp(s_ref[span(k)] - peak)
                s_ref[span(k)] = e
                t_ref[span(k)] = d
                total += jnp.sum(e, axis=0, keepdims=True)
                weighted += jnp.sum(e * d, axis=0, keepdims=True)
            inverse = 1.0 / total
            delta = weighted * inverse
            near_scale = shrink * inverse
            for k in range(i, i + 5):
                if k < 2:
                    p, d = s_ref[span(k)] * inverse, t_ref[span(k)]
                else:
                    p, d = e_ref[step, span(k - 2)] * near_scale, d_ref[step, span(k - 2)]
                p_ref[step, span(k - i)] = p.astype(BF)
                ds = (p * (d - delta)).astype(BF)
                acc[span(k)] += jnp.dot(ds, q, preferred_element_type=F32)

    dk2[...] = acc[0:rows].astype(BF)
    dk1[...] = acc[rows : 2 * rows].astype(BF)
    dk0[...] = acc[2 * rows : 3 * rows]


def values_body(p_ref, own, e1, e2, o_ref):
    tn = (((0,), (0,)), ((), ()))
    for i in range(2):
        value = jnp.concatenate(
            [e2[i * TILE :, HEAD_SIZE:], e1[:, HEAD_SIZE:], own[: (i + 1) * TILE, HEAD_SIZE:]], axis=0
        )
        for h in range(2):
            a = lax.dot_general(p_ref[2 * h + i], value, tn, preferred_element_type=F32)
            o_ref[i * TILE : (i + 1) * TILE, h * HEAD_SIZE : (h + 1) * HEAD_SIZE] = a.astype(BF)


def attend(lens, query, own, e1, e2, grad):
    rows = query.shape[0]
    full = pl.BlockSpec(memory_space=pltpu.VMEM)
    shape = jax.ShapeDtypeStruct
    pairs = 4 * TILE * REACH
    e, d, stat = pl.pallas_call(
        near_body,
        out_shape=(
            shape((4, 2 * rows, TILE), F32),
            shape((4, 2 * rows, TILE), F32),
            shape((4, 8, TILE), F32),
        ),
        in_specs=[full] * 5,
        out_specs=(full,) * 3,
        cost_estimate=pl.CostEstimate(
            flops=3 * pairs * HEAD_SIZE, bytes_accessed=5 * rows * 1024 + 8 * pairs, transcendentals=pairs
        ),
        compiler_params=pltpu.CompilerParams(vmem_limit_bytes=16 * MIB),
        name="near_scores",
    )(lens, query, own, e1, grad)
    p, dk0, dk1, dk2 = pl.pallas_call(
        far_body,
        out_shape=(
            shape((4, REACH, TILE), BF),
            shape((rows, HEAD_SIZE), F32),
            shape((rows, HEAD_SIZE), BF),
            shape((rows, HEAD_SIZE), BF),
        ),
        in_specs=[full] * 7,
        out_specs=(full,) * 4,
        scratch_shapes=[
            pltpu.VMEM((rows, TILE), F32),
            pltpu.VMEM((rows, TILE), F32),
            pltpu.VMEM((3 * rows, HEAD_SIZE), F32),
        ],
        cost_estimate=pl.CostEstimate(
            flops=3 * pairs * HEAD_SIZE, bytes_accessed=5 * rows * 1024 + 10 * pairs, transcendentals=pairs
        ),
        compiler_params=pltpu.CompilerParams(vmem_limit_bytes=20 * MIB),
        name="far_scores",
    )(lens, query, e2, grad, e, d, stat)
    out = pl.pallas_call(
        values_body,
        out_shape=shape((rows, 2 * HEAD_SIZE), BF),
        in_specs=[full] * 4,
        out_specs=full,
        cost_estimate=pl.CostEstimate(
            flops=2 * pairs * HEAD_SIZE, bytes_accessed=4 * rows * 1024 + 2 * pairs, transcendentals=0
        ),
        compiler_params=pltpu.CompilerParams(vmem_limit_bytes=14 * MIB),
        name="values",
    )(p, own, e1, e2)
    return out, dk0, dk1, dk2


def local(tokens, w_query, key_matrix, value_matrix, d_attended, doc_lengths):
    feature = jnp.arange(tokens.shape[1], dtype=jnp.int32)
    target = feature // ROWS * PAD + feature % ROWS
    spread = (target[:, None] == jnp.arange(8 * PAD, dtype=jnp.int32)[None, :]).astype(BF)
    own = jnp.dot(tokens, spread, preferred_element_type=F32).astype(BF)

    partner = hop(own, dz=NZL)
    near = ring_x(own)
    far = ring_x(partner)

    w = gather_zcore(jnp.concatenate([key_matrix, value_matrix, w_query], axis=1))
    w = jnp.pad(w, ((0, 0), (0, PAD - ROWS), (0, 0)))
    kv_own, q_own = split(w)
    kv_one, q_one = split(hop(w, dy=1, by_core=True))
    kv = ring_y(kv_own, kv_one)
    kv_a = hop(joined_blocks(kv[1:4]), swap=1)
    qs = ring_y(q_own, q_one)
    q_a = hop(joined_blocks(qs[1:4]), swap=1)

    sums = project(near, far, kv, kv_a, 1.0, slots=(0, 1, 3), dtype=F32)
    joined = project(near, far, kv, kv_a, 1.0, slots=(2,), sums=(sums,))
    query = project(near, far, qs, q_a, 0.0625)

    e2 = along_ctx(joined, 2)
    e1 = along_ctx(joined, 1)
    attended, dk0, dk1, dk2 = attend(
        doc_lengths.reshape(1, -1), query, joined, e1, e2, d_attended
    )
    key_total = dk0 + along_ctx(dk2, -2).astype(F32) + along_ctx(dk1, -1).astype(F32)
    return (attended, key_total.astype(BF))


def solution(mesh):
    return jax.shard_map(
        local,
        mesh=mesh,
        in_specs=(
            P("ctx", "head"),
            P("ctx", "head"),
            P("ctx", "head"),
            P("ctx", "head"),
            P("ctx", "head"),
            P(),
        ),
        out_specs=(P("ctx", "head"), P("ctx", "head")),
        check_vma=False,
    )
```
